512 devices in a mesh: section: 8 (over x_lo, y), seq: 64 (over x_hi, z, core).
Axes of the slice: x: 4 (x_hi: 2, x_lo: 2; x = x_hi * 2 + x_lo), y: 4, z: 16, core: 2. Of those that a mesh axis runs over, the one named last changes fastest.
Arguments:
- resident_microbatches: bfloat16 [8, 8192, 1024], P('section', 'seq'), may hold values from -64 to 64
- arriving_microbatch: bfloat16 [8192, 1024], P('seq'), may hold values from -64 to 64
- prenormal_scaling: float32 [8, 1024], P('section'), may hold values from 0.1 to 1.9
- attention_triple_matrix: bfloat16 [8, 1024, 3072], P('section', 'seq'), may hold values from -0.1875 to 0.1875
- exit_projection_matrix: bfloat16 [8, 1024, 1024], P('section'), may hold values from -0.1875 to 0.1875
- mirrored_lookup_tile: int32 [64, 4], replicated, may hold values from 0 to 1
Outputs:
- tick_out: bfloat16 [2, 8, 8192, 1024], P(None, 'section', 'seq')
The draws below stay inside these ranges and needn't reach their ends.
All inputs are finite; a program needn't handle non-finite values.
Results may differ from the reference program's by a relative error of at most 0.004.
Values may be sent and summed in bfloat16 or wider, within the bound.
A program may use at most 64 MiB of HBM per device.

```python
import math
import jax
import jax.numpy as jnp
from jax import lax

D = 1024
HEADS = 8
HEAD = 128
BLOCK = 64
LEVELS = 4
TOK_DEV = 128
INNER = 1024
BLK_DEV = 2
TOKENS = 8192
SECTIONS = 8
N_SEQ = 64


def scaled_field(key, lead, row_count, col_count):
    first_key, second_key, third_key = jax.random.split(key, 3)
    log_low = math.log(0.3)
    log_high = math.log(3.0)
    col_scale = jnp.exp(jax.random.uniform(first_key, (lead, 1, col_count), jnp.float32, log_low, log_high))
    row_scale = jnp.exp(jax.random.uniform(second_key, (lead, row_count, 1), jnp.float32, log_low, log_high))
    base = jnp.clip(jax.random.normal(third_key, (lead, row_count, col_count), jnp.float32), -6.0, 6.0)
    return base * row_scale * col_scale


def draw_resident_microbatches(key, part):
    return scaled_field(jax.random.fold_in(key, 11), SECTIONS, TOKENS, D).astype(jnp.bfloat16)


def draw_arriving_microbatch(key, part):
    return scaled_field(jax.random.fold_in(key, 23), 1, TOKENS, D)[0].astype(jnp.bfloat16)


def place_ends(values, stream_key, least, top_value):
    spot = [jax.random.randint(jax.random.fold_in(stream_key, axis), (), 0, length) for axis, length in enumerate(values.shape)]
    main_axis = values.shape.index(max(values.shape))
    beside = spot[:main_axis] + [(spot[main_axis] + 1) % values.shape[main_axis]] + spot[main_axis + 1:]
    return values.at[tuple(spot)].set(least).at[tuple(beside)].set(top_value)


def levels(rng, shape, pieces, smallest, high):
    def one(dim, shards_of):
        heights = jax.random.uniform(jax.random.fold_in(jax.random.fold_in(rng, 6), dim), (shards_of,), jnp.float32, smallest / len(pieces), high / len(pieces))
        return jnp.repeat(jnp.exp(heights), shape[dim] // shards_of).reshape((-1,) + (1,) * (len(shape) - dim - 1))

    loudness = one(*pieces[0])
    for cut in pieces[1:]:
        loudness = loudness * one(*cut)
    return loudness


def scatter_about(stream_key, extent, scale, bound, pieces=(), held_as=jnp.bfloat16):
    entries = scale * jax.random.normal(stream_key, extent, jnp.float32)
    if pieces:
        entries = entries * levels(stream_key, extent, pieces, -0.22, 0.18)
    return jnp.clip(entries, -bound, bound).astype(held_as)


def setup_inputs(seed: int = 0) -> dict:
    key_list = jax.random.split(jax.random.key(seed), 7)
    return {
        "resident_microbatches": draw_resident_microbatches(jax.random.fold_in(key_list[6], 71), 0),
        "arriving_microbatch": draw_arriving_microbatch(jax.random.fold_in(key_list[6], 71), 0),
        "prenormal_scaling": jnp.clip(1.0 + 0.18 * jax.random.normal(key_list[2], (SECTIONS, D), jnp.float32), 0.1, 1.9),
        "attention_triple_matrix": scatter_about(key_list[3], (SECTIONS, D, 3 * INNER), D ** -0.5, 0.1875, ((0, 8), (1, 64))),
        "exit_projection_matrix": scatter_about(key_list[4], (SECTIONS, INNER, D), INNER ** -0.5, 0.1875, ((0, 8),)),
        "mirrored_lookup_tile": place_ends(jax.random.randint(key_list[5], (N_SEQ, LEVELS), 0, BLK_DEV), jax.random.fold_in(key_list[5], 1), 0, BLK_DEV - 1).astype(jnp.int32),
    }


epsilon = 1e-06

def head_norm(projected, row_count):
    shaped = projected.reshape(row_count, HEADS, HEAD)
    mean_square = lax.optimization_barrier(jnp.mean(shaped * shaped, axis=-1, keepdims=True))
    return (shaped * lax.rsqrt(mean_square + epsilon)).astype(jnp.bfloat16)

def attend_device(operands):
    queries, own_keys, own_values, far_keys, far_values = operands
    blocks = queries.shape[0]
    score_scale = HEAD ** (-0.5)
    far_keys = jnp.broadcast_to(far_keys.reshape(1, LEVELS * BLOCK, HEADS, HEAD), (blocks, LEVELS * BLOCK, HEADS, HEAD))
    far_values = jnp.broadcast_to(far_values.reshape(1, LEVELS * BLOCK, HEADS, HEAD), (blocks, LEVELS * BLOCK, HEADS, HEAD))
    all_keys = jnp.concatenate([own_keys, far_keys], axis=1)
    all_values = jnp.concatenate([own_values, far_values], axis=1)
    scores = jnp.einsum('cqhd,ckhd->chqk', queries.astype(jnp.float32), all_keys.astype(jnp.float32)) * score_scale
    exps = jnp.exp(scores)
    weights = (exps / lax.optimization_barrier(jnp.sum(exps, axis=-1, keepdims=True))).astype(jnp.bfloat16)
    mixed_heads = jnp.einsum('chqk,ckhd->cqhd', weights.astype(jnp.float32), all_values.astype(jnp.float32))
    return mixed_heads.astype(jnp.bfloat16)

def transform_through_tier(hidden_in, gain_row, weights, out_weights, mirrored_lookup_tile):
    inner_width = HEADS * HEAD
    blocks = TOK_DEV // BLOCK
    widened = hidden_in.astype(jnp.float32)
    mean_square = lax.optimization_barrier(jnp.mean(widened * widened, axis=-1, keepdims=True))
    normed = (widened * lax.rsqrt(mean_square + epsilon) * gain_row.astype(jnp.float32)).astype(jnp.bfloat16)
    projected = jnp.dot(normed, weights, preferred_element_type=jnp.float32)
    queries = head_norm(projected[:, :inner_width], TOKENS)
    key_rows = head_norm(projected[:, inner_width:2 * inner_width], TOKENS)
    values = projected[:, 2 * inner_width:].astype(jnp.bfloat16).reshape(TOKENS, HEADS, HEAD)
    query_blocks = queries.reshape(N_SEQ, blocks, BLOCK, HEADS, HEAD)
    key_blocks = key_rows.reshape(N_SEQ, blocks, BLOCK, HEADS, HEAD)
    value_blocks = values.reshape(N_SEQ, blocks, BLOCK, HEADS, HEAD)
    devices = jnp.arange(N_SEQ, dtype=jnp.int32)
    partners = jnp.stack([jnp.bitwise_xor(devices, jnp.int32(1 << bit_level)) for bit_level in range(LEVELS)], axis=1)
    chosen = mirrored_lookup_tile.astype(jnp.int32)
    far_keys = key_blocks[partners, chosen]
    far_values = value_blocks[partners, chosen]
    attended = lax.map(attend_device, (query_blocks, key_blocks, value_blocks, far_keys, far_values))
    attended = attended.reshape(TOKENS, inner_width)
    return (widened + jnp.dot(attended, out_weights, preferred_element_type=jnp.float32)).astype(jnp.bfloat16)

def reference(resident_microbatches, arriving_microbatch, prenormal_scaling, attention_triple_matrix, exit_projection_matrix, mirrored_lookup_tile):
    starting_result = []
    for tier_ordinal in range(SECTIONS):
        starting_result.append(transform_through_tier(resident_microbatches[tier_ordinal], prenormal_scaling[tier_ordinal], attention_triple_matrix[tier_ordinal], exit_projection_matrix[tier_ordinal], mirrored_lookup_tile))
    second_in = [arriving_microbatch] + starting_result[:-1]
    second_out = []
    for tier_ordinal in range(SECTIONS):
        second_out.append(transform_through_tier(second_in[tier_ordinal], prenormal_scaling[tier_ordinal], attention_triple_matrix[tier_ordinal], exit_projection_matrix[tier_ordinal], mirrored_lookup_tile))
    return jnp.stack([jnp.stack(starting_result), jnp.stack(second_out)])
```

```python
import jax
import jax.numpy as jnp
from jax import lax
from jax.experimental import pallas as pl
from jax.experimental.pallas import tpu as pltpu
from jax.sharding import PartitionSpec as P

HEADS = 8
HEAD = 128
BLOCK = 64
LEVELS = 4
NZ = 16
RUN = 128
D = 1024
INNER = 1024
SHARD = 16
PASSES = 4
PCOLS = 768
PW = 256
ROWS = RUN + LEVELS * BLOCK
EPS = 1e-06

BOTH = (False, False, False, False)


def flip(i, bit):
    step = 1 << bit
    return i + step * (1 - 2 * ((i // step) % 2))


def kernel(
    sections,
    x_hbm,
    arr_hbm,
    gain_ref,
    w_hbm,
    wo_hbm,
    table_ref,
    out_hbm,
    wbuf,
    wo,
    x1,
    x2,
    arr,
    nrm,
    att,
    send1,
    send2,
    o1,
    o2,
    rbuf,
    load_sem,
    z_recv,
    x_recv,
    sib_recv,
    z_send,
    x_send,
    sib_send,
    e_send,
    e_recv,
    r_send,
    r_recv,
    out_sem,
):
    sec = lax.axis_index("section")
    me = lax.axis_index("seq")
    h = me // (2 * NZ)
    z = (me // 2) % NZ
    c = me % 2
    nxt = (sec + 1) % sections
    prv = (sec + sections - 1) % sections

    def at(hh, zz, cc):
        return hh * (2 * NZ) + zz * 2 + cc

    up = at(h, (z + 1) % NZ, c)
    down = at(h, (z + NZ - 1) % NZ, c)
    sib = flip(me, 0)
    across = at(1 - h, z, c)
    partners = [flip(me, b) for b in range(LEVELS)]

    def dev(s, j):
        return {"section": s, "seq": j}

    barrier = pltpu.get_barrier_semaphore()
    talk = [(sec, up), (sec, down), (sec, sib), (sec, across)]
    talk += [(sec, partners[b]) for b in range(1, LEVELS)]
    talk += [(prv, me)] + [(prv, partners[b]) for b in range(1, LEVELS)]
    for s, j in talk:
        pl.semaphore_signal(barrier, inc=1, device_id=dev(s, j))

    def choose(ref, reader, level):
        second = jnp.full((BLOCK, D), table_ref[reader, level], jnp.int32) > 0
        lower = ref[pl.ds(0, BLOCK), :].astype(jnp.float32)
        upper = ref[pl.ds(BLOCK, BLOCK), :].astype(jnp.float32)
        return jnp.where(second, upper, lower).astype(jnp.bfloat16)

    def rows(slot):
        return pl.ds(pl.multiple_of(slot * SHARD, SHARD), SHARD)

    loads = []
    for p in range(PASSES):
        for g in range(3):
            loads.append(
                pltpu.make_async_copy(
                    w_hbm.at[0, :, pl.ds(g * INNER + p * PW, PW)],
                    wbuf.at[rows(me), pl.ds(p * PCOLS + g * PW, PW)],
                    load_sem.at[p * 3 + g],
                )
            )
    load_x = pltpu.make_async_copy(x_hbm.at[0], x1.at[pl.ds(0, RUN)], load_sem.at[12])
    load_arr = pltpu.make_async_copy(arr_hbm, arr, load_sem.at[13])
    load_wo = pltpu.make_async_copy(wo_hbm.at[0], wo, load_sem.at[14])
    load_x.start()
    for cp in loads:
        cp.start()
    load_arr.start()
    load_wo.start()
    load_x.wait()
    for b in range(LEVELS):
        send1[b] = choose(x1, partners[b], b)
    for cp in loads:
        cp.wait()
    pl.semaphore_wait(barrier, len(talk))

    def cols(p):
        return pl.ds(p * PCOLS, PCOLS)

    def piece(slot, p):
        return wbuf.at[rows(slot), cols(p)]

    def push(slot, p, send, recv, target):
        pltpu.make_async_remote_copy(
            src_ref=piece(slot, p),
            dst_ref=piece(slot, p),
            send_sem=send,
            recv_sem=recv,
            device_id=dev(sec, target),
        ).start()

    def got(slot, p, recv):
        pltpu.make_async_copy(piece(slot, p), piece(slot, p), recv).wait()

    def to_sib(slot, p):
        push(slot, p, sib_send.at[p], sib_recv.at[p], sib)

    def zsem(col, d, s, p):
        return z_recv.at[((col * 2 + d) * 9 + s) * PASSES + p]

    def xsem(s, d, p):
        return x_recv.at[(d * 9 + s) * PASSES + p]

    def exch(b, src, dst, send, recv, s, j):
        return pltpu.make_async_remote_copy(
            src_ref=src, dst_ref=dst, send_sem=send, recv_sem=recv, device_id=dev(s, j)
        )

    e1 = [
        exch(
            b,
            send1.at[b],
            x1.at[pl.ds(RUN + b * BLOCK, BLOCK)],
            e_send.at[b],
            e_recv.at[b],
            sec,
            partners[b],
        )
        for b in range(LEVELS)
    ]

    for p in range(PASSES):
        push(me, p, z_send.at[p], zsem(0, 0, 1, p), up)
        push(me, p, z_send.at[p], zsem(0, 1, 1, p), down)
        to_sib(me, p)
        push(me, p, x_send.at[p], xsem(0, 0, p), across)
    for b in range(LEVELS):
        e1[b].start()

    for p in range(PASSES):
        if BOTH[p]:
            got(across, p, xsem(0, 0, p))
            push(across, p, z_send.at[p], zsem(1, 0, 1, p), up)
            push(across, p, z_send.at[p], zsem(1, 1, 1, p), down)
            to_sib(across, p)

    def arrivals(s, full, last):
        below = at(h, (z + NZ - s) % NZ, c)
        above = at(h, (z + s) % NZ, c)
        for p in range(PASSES):
            for col in range(2 if BOTH[p] else 1):
                shift = (1 - 2 * h) * (2 * NZ) * col
                got(below + shift, p, zsem(col, 0, s, p))
                if not last:
                    push(below + shift, p, z_send.at[p], zsem(col, 0, s + 1, p), up)
                if not BOTH[p]:
                    push(below, p, x_send.at[p], xsem(s, 0, p), across)
                to_sib(below + shift, p)
                if not last:
                    got(above + shift, p, zsem(col, 1, s, p))
                    if full:
                        push(above + shift, p, z_send.at[p], zsem(col, 1, s + 1, p), down)
                    if not BOTH[p]:
                        push(above, p, x_send.at[p], xsem(s, 1, p), across)
                    to_sib(above + shift, p)

    def crossed(s, two):
        below = at(1 - h, (z + NZ - s) % NZ, c)
        above = at(1 - h, (z + s) % NZ, c)
        for p in range(PASSES):
            if not BOTH[p]:
                got(below, p, xsem(s, 0, p))
                to_sib(below, p)
                if two:
                    got(above, p, xsem(s, 1, p))
                    to_sib(above, p)

    def step(s, carry):
        arrivals(s, True, False)

        @pl.when(s == 1)
        def _():
            crossed(0, False)

        @pl.when(s > 1)
        def _():
            crossed(s - 1, True)

        return carry

    lax.fori_loop(1, NZ // 2 - 1, step, 0)
    arrivals(NZ // 2 - 1, False, False)
    crossed(NZ // 2 - 2, True)
    arrivals(NZ // 2, False, True)
    crossed(NZ // 2 - 1, True)
    crossed(NZ // 2, False)

    qrow = lax.broadcasted_iota(jnp.int32, (RUN, ROWS), 0)
    kcol = lax.broadcasted_iota(jnp.int32, (RUN, ROWS), 1)
    seen = (kcol >= RUN) | ((kcol >= BLOCK) == (qrow >= BLOCK))
    mask = jnp.where(seen, 1.0, 0.0).astype(jnp.float32)

    def unit(a):
        ms = jnp.mean(a * a, axis=-1, keepdims=True)
        return (a * lax.rsqrt(ms + EPS)).astype(jnp.bfloat16)

    def normalise(xr, start, count):
        wide = xr[pl.ds(start, count), :].astype(jnp.float32)
        ms = jnp.mean(wide * wide, axis=-1, keepdims=True)
        nrm[pl.ds(start, count), :] = (wide * lax.rsqrt(ms + EPS) * gain_ref[...]).astype(
            jnp.bfloat16
        )

    def layer(xr, outv, tick):
        def group(p, carry):
            base = pl.multiple_of(p * PCOLS, PCOLS)
            q = jnp.dot(
                nrm[pl.ds(0, RUN), :], wbuf[:, pl.ds(base, PW)], preferred_element_type=jnp.float32
            )
            k = jnp.dot(
                nrm[...], wbuf[:, pl.ds(base + PW, PW)], preferred_element_type=jnp.float32
            )
            v = jnp.dot(
                nrm[...], wbuf[:, pl.ds(base + 2 * PW, PW)], preferred_element_type=jnp.float32
            ).astype(jnp.bfloat16)
            for i in range(PW // HEAD):
                lanes = slice(i * HEAD, (i + 1) * HEAD)
                score = lax.dot_general(
                    unit(q[:, lanes]),
                    unit(k[:, lanes]),
                    (((1,), (1,)), ((), ())),
                    preferred_element_type=jnp.float32,
                ) * (HEAD ** (-0.5))
                e = jnp.exp(score) * mask
                weight = (e / jnp.sum(e, axis=-1, keepdims=True)).astype(jnp.bfloat16)
                att[:, pl.ds(pl.multiple_of(p * PW + i * HEAD, HEAD), HEAD)] = jnp.dot(
                    weight, v[:, lanes], preferred_element_type=jnp.float32
                ).astype(jnp.bfloat16)
            return carry

        lax.fori_loop(0, PASSES, group, 0)

        def project(n, carry):
            lanes = pl.ds(pl.multiple_of(n * PW, PW), PW)
            outv[:, lanes] = (
                xr[pl.ds(0, RUN), lanes].astype(jnp.float32)
                + jnp.dot(att[...], wo[:, lanes], preferred_element_type=jnp.float32)
            ).astype(jnp.bfloat16)
            return carry

        lax.fori_loop(0, D // PW, project, 0)
        cp = pltpu.make_async_copy(outv, out_hbm.at[tick, 0], out_sem.at[tick])
        cp.start()
        return cp

    for b in range(LEVELS):
        e1[b].wait_recv()
    normalise(x1, 0, ROWS)
    for p in range(PASSES):
        half = wbuf.at[pl.ds(0, 512), cols(p)]
        pltpu.make_async_copy(half, half, sib_recv.at[p]).wait()
    load_wo.wait()
    load_arr.wait()
    out1 = layer(x1, o1, 0)

    rbuf[...] = jnp.where(sec == sections - 1, arr[...], o1[...])
    for b in range(1, LEVELS):
        send2[b] = choose(rbuf, partners[b], b)
    relay = exch(0, rbuf, x2.at[pl.ds(0, RUN)], r_send.at[4], r_recv.at[4], nxt, me)
    relay.start()
    e2 = [None] + [
        exch(
            b,
            send2.at[b],
            x2.at[pl.ds(RUN + b * BLOCK, BLOCK)],
            r_send.at[b],
            r_recv.at[b],
            nxt,
            partners[b],
        )
        for b in range(1, LEVELS)
    ]
    for b in (3, 2, 1):
        e2[b].start()
    relay.wait_recv()
    send2[0] = choose(x2, sib, 0)
    e2[0] = exch(
        0, send2.at[0], x2.at[pl.ds(RUN, BLOCK)], r_send.at[0], r_recv.at[0], sec, sib
    )
    e2[0].start()
    for b in range(LEVELS):
        e2[b].wait_recv()
    normalise(x2, 0, ROWS)
    out2 = layer(x2, o2, 1)

    for p in range(PASSES):
        zn = (2 * (NZ - 1)) if BOTH[p] else (NZ - 1)
        xn = 1 if BOTH[p] else NZ
        for n, sem in ((zn, z_send.at[p]), (xn, x_send.at[p]), (2 * NZ, sib_send.at[p])):
            ref = wbuf.at[pl.ds(0, n * SHARD), cols(p)]
            pltpu.make_async_copy(ref, ref, sem).wait()
    for b in range(LEVELS):
        e1[b].wait_send()
        e2[b].wait_send()
    relay.wait_send()
    out1.wait()
    out2.wait()


def per_device(sections, x, arr, gain, w, wo, table):
    import functools

    anyspec = pl.BlockSpec(memory_space=pl.ANY)
    vspec = pl.BlockSpec(memory_space=pltpu.VMEM)
    dma = pltpu.SemaphoreType.DMA
    bf = jnp.bfloat16
    return pl.pallas_call(
        functools.partial(kernel, sections),
        out_shape=jax.ShapeDtypeStruct((2, 1, RUN, D), bf),
        in_specs=[
            anyspec,
            anyspec,
            vspec,
            anyspec,
            anyspec,
            pl.BlockSpec(memory_space=pltpu.SMEM),
        ],
        out_specs=anyspec,
        scratch_shapes=[
            pltpu.VMEM((D, 3 * INNER), bf),
            pltpu.VMEM((INNER, D), bf),
            pltpu.VMEM((ROWS, D), bf),
            pltpu.VMEM((ROWS, D), bf),
            pltpu.VMEM((RUN, D), bf),
            pltpu.VMEM((ROWS, D), bf),
            pltpu.VMEM((RUN, INNER), bf),
            pltpu.VMEM((LEVELS, BLOCK, D), bf),
            pltpu.VMEM((LEVELS, BLOCK, D), bf),
            pltpu.VMEM((RUN, D), bf),
            pltpu.VMEM((RUN, D), bf),
            pltpu.VMEM((RUN, D), bf),
            dma((15,)),
            dma((4 * 9 * PASSES,)),
            dma((2 * 9 * PASSES,)),
            dma((PASSES,)),
            dma((PASSES,)),
            dma((PASSES,)),
            dma((PASSES,)),
            dma((LEVELS,)),
            dma((LEVELS,)),
            dma((LEVELS + 1,)),
            dma((LEVELS + 1,)),
            dma((2,)),
        ],
        compiler_params=pltpu.CompilerParams(
            collective_id=0, has_side_effects=True, vmem_limit_bytes=56 * 1024 * 1024
        ),
    )(x, arr, gain, w, wo, table)


def solution(mesh):
    import functools

    placed = (
        P("section", "seq", None),
        P("seq", None),
        P("section", None),
        P("section", "seq", None),
        P("section", None, None),
        P(),
    )
    return jax.shard_map(
        functools.partial(per_device, mesh.shape["section"]),
        mesh=mesh,
        in_specs=placed,
        out_specs=P(None, "section", "seq", None),
        check_vma=False,
    )
```

```python
import jax
import jax.numpy as jnp
from jax import lax
from jax.experimental import pallas as pl
from jax.experimental.pallas import tpu as pltpu
from jax.sharding import PartitionSpec as P

HEADS = 8
HEAD = 128
BLOCK = 64
LEVELS = 4
NZ = 16
RUN = 128
D = 1024
INNER = 1024
SHARD = 16
PASSES = 4
PCOLS = 768
PW = 256
ROWS = RUN + LEVELS * BLOCK
EPS = 1e-06

HOLD = ()
EXCHANGE_AT = (5, 5, 5)


def flip(i, bit):
    step = 1 << bit
    return i + step * (1 - 2 * ((i // step) % 2))


def kernel(
    sections,
    x_hbm,
    arr_hbm,
    gain_hbm,
    w_hbm,
    wo_hbm,
    table_hbm,
    out_hbm,
    wbuf,
    wo,
    x1,
    x2,
    arr,
    nrm,
    qn,
    kn,
    vb,
    att,
    gain_ref,
    table_ref,
    send1,
    send2,
    o1,
    o2,
    rbuf,
    load_sem,
    z_recv,
    x_recv,
    sib_recv,
    z_send,
    x_send,
    sib_send,
    e_send,
    e_recv,
    r_send,
    r_recv,
    out_sem,
):
    sec = lax.axis_index("section")
    me = lax.axis_index("seq")
    h = me // (2 * NZ)
    z = (me // 2) % NZ
    c = me % 2
    nxt = (sec + 1) % sections
    prv = (sec + sections - 1) % sections

    def at(hh, zz, cc):
        return hh * (2 * NZ) + zz * 2 + cc

    up = at(h, (z + 1) % NZ, c)
    down = at(h, (z + NZ - 1) % NZ, c)
    sib = flip(me, 0)
    across = at(1 - h, z, c)
    partners = [flip(me, b) for b in range(LEVELS)]

    def dev(s, j):
        return {"section": s, "seq": j}

    barrier = pltpu.get_barrier_semaphore()
    talk = [(sec, up), (sec, down), (sec, sib), (sec, across)]
    talk += [(sec, partners[b]) for b in range(1, LEVELS)]
    talk += [(prv, me)] + [(prv, partners[b]) for b in range(1, LEVELS)]
    for s, j in talk:
        pl.semaphore_signal(barrier, inc=1, device_id=dev(s, j))

    def choose(ref, reader, level):
        row = table_ref[pl.ds(level, 1), :].astype(jnp.float32)
        here = lax.broadcasted_iota(jnp.int32, row.shape, 1) == reader
        entry = jnp.sum(jnp.where(here, row, 0.0), axis=1, keepdims=True)
        second = jnp.broadcast_to(entry, (BLOCK, D)) > 0.5
        lower = ref[pl.ds(0, BLOCK), :].astype(jnp.float32)
        upper = ref[pl.ds(BLOCK, BLOCK), :].astype(jnp.float32)
        return jnp.where(second, upper, lower).astype(jnp.bfloat16)

    def rows(slot):
        return pl.ds(pl.multiple_of(slot * SHARD, SHARD), SHARD)

    loads = []
    for p in range(PASSES):
        for g in range(3):
            loads.append(
                pltpu.make_async_copy(
                    w_hbm.at[0, :, pl.ds(g * INNER + p * PW, PW)],
                    wbuf.at[rows(me), pl.ds(p * PCOLS + g * PW, PW)],
                    load_sem.at[p * 3 + g],
                )
            )
    load_x = pltpu.make_async_copy(x_hbm.at[0], x1.at[pl.ds(0, RUN)], load_sem.at[12])
    load_arr = pltpu.make_async_copy(arr_hbm, arr, load_sem.at[13])
    load_wo = pltpu.make_async_copy(wo_hbm.at[0], wo, load_sem.at[14])
    load_gain = pltpu.make_async_copy(gain_hbm, gain_ref, load_sem.at[15])
    load_table = pltpu.make_async_copy(table_hbm, table_ref, load_sem.at[16])
    load_table.start()
    load_x.start()
    load_gain.start()
    for cp in loads:
        cp.start()
    load_arr.start()
    load_wo.start()
    load_table.wait()
    load_x.wait()
    for b in range(LEVELS):
        send1[b] = choose(x1, partners[b], b)
    for cp in loads:
        cp.wait()
    pl.semaphore_wait(barrier, len(talk))

    def cols(p):
        return pl.ds(p * PCOLS, PCOLS)

    def piece(slot, p):
        return wbuf.at[rows(slot), cols(p)]

    def push(slot, p, send, recv, target):
        pltpu.make_async_remote_copy(
            src_ref=piece(slot, p),
            dst_ref=piece(slot, p),
            send_sem=send,
            recv_sem=recv,
            device_id=dev(sec, target),
        ).start()

    def got(slot, p, recv):
        pltpu.make_async_copy(piece(slot, p), piece(slot, p), recv).wait()

    def to_sib(slot, p):
        push(slot, p, sib_send.at[p], sib_recv.at[p], sib)

    def zsem(d, s, p):
        return z_recv.at[(d * 9 + s) * PASSES + p]

    def xsem(d, s, p):
        return x_recv.at[(d * 9 + s) * PASSES + p]

    def exch(b, src, dst, send, recv, s, j):
        return pltpu.make_async_remote_copy(
            src_ref=src, dst_ref=dst, send_sem=send, recv_sem=recv, device_id=dev(s, j)
        )

    e1 = [
        exch(
            b,
            send1.at[b],
            x1.at[pl.ds(RUN + b * BLOCK, BLOCK)],
            e_send.at[b],
            e_recv.at[b],
            sec,
            partners[b],
        )
        for b in range(LEVELS)
    ]

    def begin():
        for p in range(PASSES):
            push(me, p, z_send.at[p], zsem(0, 1, p), up)
            push(me, p, z_send.at[p], zsem(1, 1, p), down)
        for p in range(PASSES):
            if p not in HOLD:
                push(me, p, x_send.at[p], xsem(0, 0, p), across)
        for p in range(PASSES):
            to_sib(me, p)

    def held(p):
        push(me, p, x_send.at[p], xsem(0, 0, p), across)

        def one(s, carry):
            below = at(h, (z + NZ - s) % NZ, c)
            above = at(h, (z + s) % NZ, c)
            push(below, p, x_send.at[p], xsem(0, s, p), across)

            @pl.when(s < NZ // 2)
            def _():
                push(above, p, x_send.at[p], xsem(1, s, p), across)

            return carry

        lax.fori_loop(1, NZ // 2 + 1, one, 0)

    def ring(s):
        below = at(h, (z + NZ - s) % NZ, c)
        above = at(h, (z + s) % NZ, c)
        for p in range(PASSES):
            got(below, p, zsem(0, s, p))

            @pl.when(s < NZ // 2)
            def _():
                push(below, p, z_send.at[p], zsem(0, s + 1, p), up)

            if p not in HOLD:
                push(below, p, x_send.at[p], xsem(0, s, p), across)
            to_sib(below, p)

            @pl.when(s < NZ // 2)
            def _(p=p):
                got(above, p, zsem(1, s, p))

                @pl.when(s < NZ // 2 - 1)
                def _():
                    push(above, p, z_send.at[p], zsem(1, s + 1, p), down)

                if p not in HOLD:
                    push(above, p, x_send.at[p], xsem(1, s, p), across)
                to_sib(above, p)

    def crossed(p):
        got(across, p, xsem(0, 0, p))
        to_sib(across, p)

        def one(s, carry):
            below = at(1 - h, (z + NZ - s) % NZ, c)
            above = at(1 - h, (z + s) % NZ, c)
            got(below, p, xsem(0, s, p))
            to_sib(below, p)

            @pl.when(s < NZ // 2)
            def _():
                got(above, p, xsem(1, s, p))
                to_sib(above, p)

            return carry

        lax.fori_loop(1, NZ // 2 + 1, one, 0)

    begin()
    e1[0].start()

    def step(i, carry):
        ring(i)
        for b in range(1, LEVELS):

            @pl.when(i == EXCHANGE_AT[b - 1])
            def _(b=b):
                e1[b].start()

        return carry

    lax.fori_loop(1, NZ // 2 + 1, step, 0)
    for p in HOLD:
        held(p)

    qrow = lax.broadcasted_iota(jnp.int32, (RUN, ROWS), 0)
    kcol = lax.broadcasted_iota(jnp.int32, (RUN, ROWS), 1)
    seen = (kcol >= RUN) | ((kcol >= BLOCK) == (qrow >= BLOCK))
    mask = jnp.where(seen, 1.0, 0.0).astype(jnp.float32)

    def unit(a):
        ms = jnp.mean(a * a, axis=-1, keepdims=True)
        return (a * lax.rsqrt(ms + EPS)).astype(jnp.bfloat16)

    def normalise(xr, start, count):
        wide = xr[pl.ds(start, count), :].astype(jnp.float32)
        ms = jnp.mean(wide * wide, axis=-1, keepdims=True)
        nrm[pl.ds(start, count), :] = (wide * lax.rsqrt(ms + EPS) * gain_ref[...]).astype(
            jnp.bfloat16
        )

    scale = HEAD ** (-0.5)

    def lanes_of(p, i):
        return pl.ds(pl.multiple_of(p * PW + i * HEAD, HEAD), HEAD)

    def prepare(p, start, count, queries):
        base = pl.multiple_of(p * PCOLS, PCOLS)
        if queries:
            q = jnp.dot(
                nrm[pl.ds(0, RUN), :], wbuf[:, pl.ds(base, PW)], preferred_element_type=jnp.float32
            )
            for i in range(PW // HEAD):
                qn[:, lanes_of(p, i)] = unit(q[:, i * HEAD : (i + 1) * HEAD])
        part = nrm[pl.ds(start, count), :]
        k = jnp.dot(part, wbuf[:, pl.ds(base + PW, PW)], preferred_element_type=jnp.float32)
        v = jnp.dot(part, wbuf[:, pl.ds(base + 2 * PW, PW)], preferred_element_type=jnp.float32)
        for i in range(PW // HEAD):
            kn[pl.ds(start, count), lanes_of(p, i)] = unit(k[:, i * HEAD : (i + 1) * HEAD])
        vb[pl.ds(start, count), pl.ds(pl.multiple_of(p * PW, PW), PW)] = v.astype(jnp.bfloat16)

    def attend(p):
        for i in range(PW // HEAD):
            lanes = lanes_of(p, i)
            score = lax.dot_general(
                qn[:, lanes],
                kn[:, lanes],
                (((1,), (1,)), ((), ())),
                preferred_element_type=jnp.float32,
            )
            e = jnp.exp(score * scale) * mask
            weight = (e / jnp.sum(e, axis=-1, keepdims=True)).astype(jnp.bfloat16)
            att[:, lanes] = jnp.dot(
                weight, vb[:, lanes], preferred_element_type=jnp.float32
            ).astype(jnp.bfloat16)

    def finish(xr, outv, tick):
        def project(n, carry):
            lanes = pl.ds(pl.multiple_of(n * PW, PW), PW)
            outv[:, lanes] = (
                xr[pl.ds(0, RUN), lanes].astype(jnp.float32)
                + jnp.dot(att[...], wo[:, lanes], preferred_element_type=jnp.float32)
            ).astype(jnp.bfloat16)
            return carry

        lax.fori_loop(0, D // PW, project, 0)
        cp = pltpu.make_async_copy(outv, out_hbm.at[tick, 0], out_sem.at[tick])
        cp.start()
        return cp

    def tick_one(p):
        half = wbuf.at[pl.ds(0, 512), cols(p)]
        pltpu.make_async_copy(half, half, sib_recv.at[p]).wait()
        prepare(p, 0, ROWS, True)
        attend(p)

    load_gain.wait()
    soon = [p for p in range(PASSES) if p not in HOLD]
    for p in soon:
        crossed(p)
    for b in range(LEVELS):
        e1[b].wait_recv()
    normalise(x1, 0, ROWS)
    for p in soon:
        tick_one(p)
    for p in HOLD:
        crossed(p)
        tick_one(p)
    load_wo.wait()
    load_arr.wait()
    out1 = finish(x1, o1, 0)

    rbuf[...] = jnp.where(sec == sections - 1, arr[...], o1[...])
    for b in range(1, LEVELS):
        send2[b] = choose(rbuf, partners[b], b)
    relay = exch(0, rbuf, x2.at[pl.ds(0, RUN)], r_send.at[4], r_recv.at[4], nxt, me)
    relay.start()
    e2 = [None] + [
        exch(
            b,
            send2.at[b],
            x2.at[pl.ds(RUN + b * BLOCK, BLOCK)],
            r_send.at[b],
            r_recv.at[b],
            nxt,
            partners[b],
        )
        for b in range(1, LEVELS)
    ]
    for b in (3, 2, 1):
        e2[b].start()
    relay.wait_recv()
    send2[0] = choose(x2, sib, 0)
    e2[0] = exch(
        0, send2.at[0], x2.at[pl.ds(RUN, BLOCK)], r_send.at[0], r_recv.at[0], sec, sib
    )
    e2[0].start()
    EARLY = RUN + BLOCK
    e2[0].wait_recv()
    normalise(x2, 0, EARLY)

    def early(p, carry):
        prepare(p, 0, EARLY, True)
        return carry

    lax.fori_loop(0, PASSES, early, 0)
    for b in range(1, LEVELS):
        e2[b].wait_recv()
    normalise(x2, EARLY, ROWS - EARLY)

    def late(p, carry):
        prepare(p, EARLY, ROWS - EARLY, False)
        attend(p)
        return carry

    lax.fori_loop(0, PASSES, late, 0)
    out2 = finish(x2, o2, 1)

    for p in range(PASSES):
        for n, sem in ((NZ - 1, z_send.at[p]), (NZ, x_send.at[p]), (2 * NZ, sib_send.at[p])):
            ref = wbuf.at[pl.ds(0, n * SHARD), cols(p)]
            pltpu.make_async_copy(ref, ref, sem).wait()
    for b in range(LEVELS):
        e1[b].wait_send()
        e2[b].wait_send()
    relay.wait_send()
    out1.wait()
    out2.wait()


def per_device(sections, x, arr, gain, w, wo, table):
    import functools

    anyspec = pl.BlockSpec(memory_space=pl.ANY)
    dma = pltpu.SemaphoreType.DMA
    bf = jnp.bfloat16
    return pl.pallas_call(
        functools.partial(kernel, sections),
        out_shape=jax.ShapeDtypeStruct((2, 1, RUN, D), bf),
        in_specs=[anyspec] * 6,
        out_specs=anyspec,
        scratch_shapes=[
            pltpu.VMEM((D, 3 * INNER), bf),
            pltpu.VMEM((INNER, D), bf),
            pltpu.VMEM((ROWS, D), bf),
            pltpu.VMEM((ROWS, D), bf),
            pltpu.VMEM((RUN, D), bf),
            pltpu.VMEM((ROWS, D), bf),
            pltpu.VMEM((RUN, INNER), bf),
            pltpu.VMEM((ROWS, INNER), bf),
            pltpu.VMEM((ROWS, INNER), bf),
            pltpu.VMEM((RUN, INNER), bf),
            pltpu.VMEM((1, D), jnp.float32),
            pltpu.VMEM(table.shape[::-1], jnp.int32),
            pltpu.VMEM((LEVELS, BLOCK, D), bf),
            pltpu.VMEM((LEVELS, BLOCK, D), bf),
            pltpu.VMEM((RUN, D), bf),
            pltpu.VMEM((RUN, D), bf),
            pltpu.VMEM((RUN, D), bf),
            dma((17,)),
            dma((2 * 9 * PASSES,)),
            dma((2 * 9 * PASSES,)),
            dma((PASSES,)),
            dma((PASSES,)),
            dma((PASSES,)),
            dma((PASSES,)),
            dma((LEVELS,)),
            dma((LEVELS,)),
            dma((LEVELS + 1,)),
            dma((LEVELS + 1,)),
            dma((2,)),
        ],
        compiler_params=pltpu.CompilerParams(
            collective_id=0, has_side_effects=True, vmem_limit_bytes=56 * 1024 * 1024
        ),
    )(x, arr, gain, w, wo, table.T)


def solution(mesh):
    import functools

    placed = (
        P("section", "seq", None),
        P("seq", None),
        P("section", None),
        P("section", "seq", None),
        P("section", None, None),
        P(),
    )
    return jax.shard_map(
        functools.partial(per_device, mesh.shape["section"]),
        mesh=mesh,
        in_specs=placed,
        out_specs=P(None, "section", "seq", None),
        check_vma=False,
    )
```

```python
import jax
import jax.numpy as jnp
from jax import lax
from jax.experimental import pallas as pl
from jax.experimental.pallas import tpu as pltpu
from jax.sharding import PartitionSpec as P

HEADS = 8
HEAD = 128
BLOCK = 64
LEVELS = 4
NZ = 16
RUN = 128
D = 1024
INNER = 1024
SHARD = 16
PASSES = 4
PCOLS = 768
PW = 256
ROWS = RUN + LEVELS * BLOCK
EPS = 1e-06
NEAR = 2

EXCHANGE_AT = (5, 5, 5)


def flip(i, bit):
    step = 1 << bit
    return i + step * (1 - 2 * ((i // step) % 2))


def kernel(
    sections,
    x_hbm,
    arr_hbm,
    gain_hbm,
    w_hbm,
    wo_hbm,
    table_hbm,
    out_hbm,
    wbuf,
    wo,
    x1,
    x2,
    arr,
    nrm,
    qn,
    kn,
    vb,
    att,
    gain_ref,
    table_ref,
    send1,
    send2,
    o1,
    o2,
    rbuf,
    load_sem,
    z_recv,
    x_recv,
    sib_recv,
    z_send,
    x_send,
    sib_send,
    e_send,
    e_recv,
    r_send,
    r_recv,
    out_sem,
):
    sec = lax.axis_index("section")
    me = lax.axis_index("seq")
    h = me // (2 * NZ)
    z = (me // 2) % NZ
    c = me % 2
    nxt = (sec + 1) % sections
    prv = (sec + sections - 1) % sections

    def at(hh, zz, cc):
        return hh * (2 * NZ) + zz * 2 + cc

    up = at(h, (z + 1) % NZ, c)
    down = at(h, (z + NZ - 1) % NZ, c)
    sib = flip(me, 0)
    across = at(1 - h, z, c)
    partners = [flip(me, b) for b in range(LEVELS)]

    def dev(s, j):
        return {"section": s, "seq": j}

    barrier = pltpu.get_barrier_semaphore()
    talk = [(sec, up), (sec, down), (sec, sib), (sec, across)]
    talk += [(sec, partners[b]) for b in range(1, LEVELS)]
    talk += [(prv, me)] + [(prv, partners[b]) for b in range(NEAR, LEVELS)]
    for s, j in talk:
        pl.semaphore_signal(barrier, inc=1, device_id=dev(s, j))

    def choose(ref, reader, level):
        row = table_ref[pl.ds(level, 1), :].astype(jnp.float32)
        here = lax.broadcasted_iota(jnp.int32, row.shape, 1) == reader
        entry = jnp.sum(jnp.where(here, row, 0.0), axis=1, keepdims=True)
        second = jnp.broadcast_to(entry, (BLOCK, D)) > 0.5
        lower = ref[pl.ds(0, BLOCK), :].astype(jnp.float32)
        upper = ref[pl.ds(BLOCK, BLOCK), :].astype(jnp.float32)
        return jnp.where(second, upper, lower).astype(jnp.bfloat16)

    def rows(slot):
        return pl.ds(pl.multiple_of(slot * SHARD, SHARD), SHARD)

    loads = []
    for p in range(PASSES):
        for g in range(3):
            loads.append(
                pltpu.make_async_copy(
                    w_hbm.at[0, :, pl.ds(g * INNER + p * PW, PW)],
                    wbuf.at[rows(me), pl.ds(p * PCOLS + g * PW, PW)],
                    load_sem.at[p * 3 + g],
                )
            )
    load_x = pltpu.make_async_copy(x_hbm.at[0], x1.at[pl.ds(0, RUN)], load_sem.at[12])
    load_arr = pltpu.make_async_copy(arr_hbm, arr, load_sem.at[13])
    load_wo = pltpu.make_async_copy(wo_hbm.at[0], wo, load_sem.at[14])
    load_gain = pltpu.make_async_copy(gain_hbm, gain_ref, load_sem.at[15])
    load_table = pltpu.make_async_copy(table_hbm, table_ref, load_sem.at[16])
    load_table.start()
    load_x.start()
    load_gain.start()
    for cp in loads:
        cp.start()
    load_arr.start()
    load_wo.start()
    load_table.wait()
    load_x.wait()
    for b in range(LEVELS):
        send1[b] = choose(x1, partners[b], b)
    for cp in loads:
        cp.wait()
    pl.semaphore_wait(barrier, len(talk))

    def normalise(xr, start, count):
        wide = xr[pl.ds(start, count), :].astype(jnp.float32)
        ms = jnp.mean(wide * wide, axis=-1, keepdims=True)
        nrm[pl.ds(start, count), :] = (wide * lax.rsqrt(ms + EPS) * gain_ref[...]).astype(
            jnp.bfloat16
        )

    def cols(p):
        return pl.ds(p * PCOLS, PCOLS)

    def piece(slot, p):
        return wbuf.at[rows(slot), cols(p)]

    def push(slot, p, send, recv, target):
        pltpu.make_async_remote_copy(
            src_ref=piece(slot, p),
            dst_ref=piece(slot, p),
            send_sem=send,
            recv_sem=recv,
            device_id=dev(sec, target),
        ).start()

    def got(slot, p, recv):
        pltpu.make_async_copy(piece(slot, p), piece(slot, p), recv).wait()

    def to_sib(slot, p):
        push(slot, p, sib_send.at[p], sib_recv.at[p], sib)

    def zsem(d, s, p):
        return z_recv.at[(d * 9 + s) * PASSES + p]

    def xsem(d, s, p):
        return x_recv.at[(d * 9 + s) * PASSES + p]

    def exch(b, src, dst, send, recv, s, j):
        return pltpu.make_async_remote_copy(
            src_ref=src, dst_ref=dst, send_sem=send, recv_sem=recv, device_id=dev(s, j)
        )

    e1 = [
        exch(
            b,
            send1.at[b],
            x1.at[pl.ds(RUN + b * BLOCK, BLOCK)],
            e_send.at[b],
            e_recv.at[b],
            sec,
            partners[b],
        )
        for b in range(LEVELS)
    ]

    def ends(hh, s, p):
        below = at(hh, (z + NZ - s) % NZ, c)
        above = at(hh, (z + s) % NZ, c)
        return (below, above) if p % 2 == 0 else (above, below)

    def targets(p):
        return (up, down) if p % 2 == 0 else (down, up)

    def begin():
        for p in range(PASSES):
            long, short = targets(p)
            push(me, p, z_send.at[p], zsem(0, 1, p), long)
            push(me, p, z_send.at[p], zsem(1, 1, p), short)
        for p in range(PASSES):
            push(me, p, x_send.at[p], xsem(0, 0, p), across)
        for p in range(PASSES):
            to_sib(me, p)

    def ring(s):
        for p in range(PASSES):
            one, two = ends(h, s, p)
            long, short = targets(p)
            got(one, p, zsem(0, s, p))

            @pl.when(s < NZ // 2)
            def _(p=p, one=one, long=long):
                push(one, p, z_send.at[p], zsem(0, s + 1, p), long)

            push(one, p, x_send.at[p], xsem(0, s, p), across)
            to_sib(one, p)

            @pl.when(s < NZ // 2)
            def _(p=p, two=two, short=short):
                got(two, p, zsem(1, s, p))

                @pl.when(s < NZ // 2 - 1)
                def _():
                    push(two, p, z_send.at[p], zsem(1, s + 1, p), short)

                push(two, p, x_send.at[p], xsem(1, s, p), across)
                to_sib(two, p)

    def crossed(lo, hi):
        if lo == 0:
            for p in range(PASSES):
                got(across, p, xsem(0, 0, p))
                to_sib(across, p)

        def one(s, carry):
            for p in range(PASSES):
                first, second = ends(1 - h, s, p)
                got(first, p, xsem(0, s, p))
                to_sib(first, p)

                @pl.when(s < NZ // 2)
                def _(p=p, second=second):
                    got(second, p, xsem(1, s, p))
                    to_sib(second, p)

            return carry

        lax.fori_loop(max(lo, 1), hi, one, 0)

    begin()
    e1[0].start()
    load_gain.wait()
    normalise(x1, 0, RUN)

    def step(i, carry):
        ring(i)
        for b in range(1, LEVELS):

            @pl.when(i == EXCHANGE_AT[b - 1])
            def _(b=b):
                e1[b].start()

        return carry

    lax.fori_loop(1, NZ // 2 + 1, step, 0)
    crossed(0, 5)

    qrow = lax.broadcasted_iota(jnp.int32, (RUN, ROWS), 0)
    kcol = lax.broadcasted_iota(jnp.int32, (RUN, ROWS), 1)
    seen = (kcol >= RUN) | ((kcol >= BLOCK) == (qrow >= BLOCK))
    mask = jnp.where(seen, 1.0, 0.0).astype(jnp.float32)

    def unit(a):
        ms = jnp.mean(a * a, axis=-1, keepdims=True)
        return (a * lax.rsqrt(ms + EPS)).astype(jnp.bfloat16)

    scale = HEAD ** (-0.5)

    def lanes_of(p, i):
        return pl.ds(pl.multiple_of(p * PW + i * HEAD, HEAD), HEAD)

    def prepare(p, start, count, queries):
        base = pl.multiple_of(p * PCOLS, PCOLS)
        if queries:
            q = jnp.dot(
                nrm[pl.ds(0, RUN), :], wbuf[:, pl.ds(base, PW)], preferred_element_type=jnp.float32
            )
            for i in range(PW // HEAD):
                qn[:, lanes_of(p, i)] = unit(q[:, i * HEAD : (i + 1) * HEAD])
        part = nrm[pl.ds(start, count), :]
        k = jnp.dot(part, wbuf[:, pl.ds(base + PW, PW)], preferred_element_type=jnp.float32)
        v = jnp.dot(part, wbuf[:, pl.ds(base + 2 * PW, PW)], preferred_element_type=jnp.float32)
        for i in range(PW // HEAD):
            kn[pl.ds(start, count), lanes_of(p, i)] = unit(k[:, i * HEAD : (i + 1) * HEAD])
        vb[pl.ds(start, count), pl.ds(pl.multiple_of(p * PW, PW), PW)] = v.astype(jnp.bfloat16)

    def attend(p):
        for i in range(PW // HEAD):
            lanes = lanes_of(p, i)
            score = lax.dot_general(
                qn[:, lanes],
                kn[:, lanes],
                (((1,), (1,)), ((), ())),
                preferred_element_type=jnp.float32,
            )
            e = jnp.exp(score * scale) * mask
            weight = (e / jnp.sum(e, axis=-1, keepdims=True)).astype(jnp.bfloat16)
            att[:, lanes] = jnp.dot(
                weight, vb[:, lanes], preferred_element_type=jnp.float32
            ).astype(jnp.bfloat16)

    def finish(xr, outv, tick):
        def project(n, carry):
            lanes = pl.ds(pl.multiple_of(n * PW, PW), PW)
            outv[:, lanes] = (
                xr[pl.ds(0, RUN), lanes].astype(jnp.float32)
                + jnp.dot(att[...], wo[:, lanes], preferred_element_type=jnp.float32)
            ).astype(jnp.bfloat16)
            return carry

        lax.fori_loop(0, D // PW, project, 0)
        cp = pltpu.make_async_copy(outv, out_hbm.at[tick, 0], out_sem.at[tick])
        cp.start()
        return cp

    def tick_one(p):
        half = wbuf.at[pl.ds(0, 512), cols(p)]
        pltpu.make_async_copy(half, half, sib_recv.at[p]).wait()
        prepare(p, 0, ROWS, True)
        attend(p)

    for b in range(LEVELS):
        e1[b].wait_recv()
    normalise(x1, RUN, ROWS - RUN)
    crossed(5, NZ // 2 + 1)
    for p in range(PASSES):
        tick_one(p)
    load_wo.wait()
    load_arr.wait()
    out1 = finish(x1, o1, 0)

    rbuf[...] = jnp.where(sec == sections - 1, arr[...], o1[...])
    for b in range(NEAR, LEVELS):
        send2[b] = choose(rbuf, partners[b], b)
    relay = exch(0, rbuf, x2.at[pl.ds(0, RUN)], r_send.at[4], r_recv.at[4], nxt, me)
    relay.start()
    e2 = [
        exch(
            b,
            send2.at[b],
            x2.at[pl.ds(RUN + b * BLOCK, BLOCK)],
            r_send.at[b],
            r_recv.at[b],
            sec if b < NEAR else nxt,
            partners[b],
        )
        for b in range(LEVELS)
    ]
    for b in range(LEVELS - 1, NEAR - 1, -1):
        e2[b].start()
    relay.wait_recv()
    for b in range(NEAR - 1, -1, -1):
        send2[b] = choose(x2, partners[b], b)
        e2[b].start()
    EARLY = RUN + BLOCK
    e2[0].wait_recv()
    normalise(x2, 0, EARLY)

    def early(p, carry):
        prepare(p, 0, EARLY, True)
        return carry

    lax.fori_loop(0, PASSES, early, 0)
    for b in range(1, LEVELS):
        e2[b].wait_recv()
    normalise(x2, EARLY, ROWS - EARLY)

    def late(p, carry):
        prepare(p, EARLY, ROWS - EARLY, False)
        attend(p)
        return carry

    lax.fori_loop(0, PASSES, late, 0)
    out2 = finish(x2, o2, 1)

    for p in range(PASSES):
        for n, sem in ((NZ - 1, z_send.at[p]), (NZ, x_send.at[p]), (2 * NZ, sib_send.at[p])):
            ref = wbuf.at[pl.ds(0, n * SHARD), cols(p)]
            pltpu.make_async_copy(ref, ref, sem).wait()
    for b in range(LEVELS):
        e1[b].wait_send()
        e2[b].wait_send()
    relay.wait_send()
    out1.wait()
    out2.wait()


def per_device(sections, x, arr, gain, w, wo, table):
    import functools

    anyspec = pl.BlockSpec(memory_space=pl.ANY)
    dma = pltpu.SemaphoreType.DMA
    bf = jnp.bfloat16
    return pl.pallas_call(
        functools.partial(kernel, sections),
        out_shape=jax.ShapeDtypeStruct((2, 1, RUN, D), bf),
        in_specs=[anyspec] * 6,
        out_specs=anyspec,
        scratch_shapes=[
            pltpu.VMEM((D, 3 * INNER), bf),
            pltpu.VMEM((INNER, D), bf),
            pltpu.VMEM((ROWS, D), bf),
            pltpu.VMEM((ROWS, D), bf),
            pltpu.VMEM((RUN, D), bf),
            pltpu.VMEM((ROWS, D), bf),
            pltpu.VMEM((RUN, INNER), bf),
            pltpu.VMEM((ROWS, INNER), bf),
            pltpu.VMEM((ROWS, INNER), bf),
            pltpu.VMEM((RUN, INNER), bf),
            pltpu.VMEM((1, D), jnp.float32),
            pltpu.VMEM(table.shape[::-1], jnp.int32),
            pltpu.VMEM((LEVELS, BLOCK, D), bf),
            pltpu.VMEM((LEVELS, BLOCK, D), bf),
            pltpu.VMEM((RUN, D), bf),
            pltpu.VMEM((RUN, D), bf),
            pltpu.VMEM((RUN, D), bf),
            dma((17,)),
            dma((2 * 9 * PASSES,)),
            dma((2 * 9 * PASSES,)),
            dma((PASSES,)),
            dma((PASSES,)),
            dma((PASSES,)),
            dma((PASSES,)),
            dma((LEVELS,)),
            dma((LEVELS,)),
            dma((LEVELS + 1,)),
            dma((LEVELS + 1,)),
            dma((2,)),
        ],
        compiler_params=pltpu.CompilerParams(
            collective_id=0, has_side_effects=True, vmem_limit_bytes=56 * 1024 * 1024
        ),
    )(x, arr, gain, w, wo, table.T)


def solution(mesh):
    import functools

    placed = (
        P("section", "seq", None),
        P("seq", None),
        P("section", None),
        P("section", "seq", None),
        P("section", None, None),
        P(),
    )
    return jax.shard_map(
        functools.partial(per_device, mesh.shape["section"]),
        mesh=mesh,
        in_specs=placed,
        out_specs=P(None, "section", "seq", None),
        check_vma=False,
    )
```

```python
import jax
import jax.numpy as jnp
from jax import lax
from jax.experimental import pallas as pl
from jax.experimental.pallas import tpu as pltpu
from jax.sharding import PartitionSpec as P

HEADS = 8
HEAD = 128
BLOCK = 64
LEVELS = 4
NZ = 16
RUN = 128
D = 1024
INNER = 1024
SHARD = 16
PASSES = 4
PCOLS = 768
PW = 256
ROWS = RUN + LEVELS * BLOCK
EPS = 1e-06
NEAR = 2
PARTS = 2
PART = D // PARTS

EXCHANGE_AT = (5, 5, 5)


def flip(i, bit):
    step = 1 << bit
    return i + step * (1 - 2 * ((i // step) % 2))


def kernel(
    sections,
    x_hbm,
    arr_hbm,
    gain_hbm,
    w_hbm,
    wo_hbm,
    table_hbm,
    out_ref,
    wbuf,
    wo,
    x1,
    x2,
    arr,
    nrm,
    qn,
    kn,
    vb,
    att,
    gain_ref,
    table_ref,
    send1,
    send2,
    rbuf,
    load_sem,
    z_recv,
    x_recv,
    sib_recv,
    z_send,
    x_send,
    sib_send,
    e_send,
    e_recv,
    r_send,
    r_recv,
):
    sec = lax.axis_index("section")
    me = lax.axis_index("seq")
    h = me // (2 * NZ)
    z = (me // 2) % NZ
    c = me % 2
    nxt = (sec + 1) % sections
    prv = (sec + sections - 1) % sections

    def at(hh, zz, cc):
        return hh * (2 * NZ) + zz * 2 + cc

    up = at(h, (z + 1) % NZ, c)
    down = at(h, (z + NZ - 1) % NZ, c)
    sib = flip(me, 0)
    across = at(1 - h, z, c)
    partners = [flip(me, b) for b in range(LEVELS)]

    def dev(s, j):
        return {"section": s, "seq": j}

    barrier = pltpu.get_barrier_semaphore()
    talk = [(sec, up), (sec, down), (sec, sib), (sec, across)]
    talk += [(sec, partners[b]) for b in range(1, LEVELS)]
    talk += [(prv, me)] + [(prv, partners[b]) for b in range(NEAR, LEVELS)]
    for s, j in talk:
        pl.semaphore_signal(barrier, inc=1, device_id=dev(s, j))

    def choose(ref, reader, level, lanes):
        row = table_ref[pl.ds(level, 1), :].astype(jnp.float32)
        here = lax.broadcasted_iota(jnp.int32, row.shape, 1) == reader
        entry = jnp.sum(jnp.where(here, row, 0.0), axis=1, keepdims=True)
        lower = ref[pl.ds(0, BLOCK), lanes].astype(jnp.float32)
        upper = ref[pl.ds(BLOCK, BLOCK), lanes].astype(jnp.float32)
        second = jnp.broadcast_to(entry, lower.shape) > 0.5
        return jnp.where(second, upper, lower).astype(jnp.bfloat16)

    def rows(slot):
        return pl.ds(pl.multiple_of(slot * SHARD, SHARD), SHARD)

    loads = []
    for p in range(PASSES):
        for g in range(3):
            loads.append(
                pltpu.make_async_copy(
                    w_hbm.at[0, :, pl.ds(g * INNER + p * PW, PW)],
                    wbuf.at[rows(me), pl.ds(p * PCOLS + g * PW, PW)],
                    load_sem.at[p * 3 + g],
                )
            )
    load_x = pltpu.make_async_copy(x_hbm.at[0], x1.at[pl.ds(0, RUN)], load_sem.at[12])
    load_arr = pltpu.make_async_copy(arr_hbm, arr, load_sem.at[13])
    load_wo = pltpu.make_async_copy(wo_hbm.at[0], wo, load_sem.at[14])
    load_gain = pltpu.make_async_copy(gain_hbm, gain_ref, load_sem.at[15])
    load_table = pltpu.make_async_copy(table_hbm, table_ref, load_sem.at[16])
    load_table.start()
    load_x.start()
    load_gain.start()
    for cp in loads:
        cp.start()
    load_arr.start()
    load_wo.start()
    load_table.wait()
    load_x.wait()
    for b in range(LEVELS):
        send1[b] = choose(x1, partners[b], b, slice(None))
    for cp in loads:
        cp.wait()
    pl.semaphore_wait(barrier, len(talk))

    def normalise(xr, start, count):
        wide = xr[pl.ds(start, count), :].astype(jnp.float32)
        ms = jnp.mean(wide * wide, axis=-1, keepdims=True)
        nrm[pl.ds(start, count), :] = (wide * lax.rsqrt(ms + EPS) * gain_ref[...]).astype(
            jnp.bfloat16
        )

    def cols(p):
        return pl.ds(p * PCOLS, PCOLS)

    def piece(slot, p):
        return wbuf.at[rows(slot), cols(p)]

    def push(slot, p, send, recv, target):
        pltpu.make_async_remote_copy(
            src_ref=piece(slot, p),
            dst_ref=piece(slot, p),
            send_sem=send,
            recv_sem=recv,
            device_id=dev(sec, target),
        ).start()

    def got(slot, p, recv):
        pltpu.make_async_copy(piece(slot, p), piece(slot, p), recv).wait()

    def to_sib(slot, p):
        push(slot, p, sib_send.at[p], sib_recv.at[p], sib)

    def zsem(d, s, p):
        return z_recv.at[(d * 9 + s) * PASSES + p]

    def xsem(d, s, p):
        return x_recv.at[(d * 9 + s) * PASSES + p]

    def exch(b, src, dst, send, recv, s, j):
        return pltpu.make_async_remote_copy(
            src_ref=src, dst_ref=dst, send_sem=send, recv_sem=recv, device_id=dev(s, j)
        )

    e1 = [
        exch(
            b,
            send1.at[b],
            x1.at[pl.ds(RUN + b * BLOCK, BLOCK)],
            e_send.at[b],
            e_recv.at[b],
            sec,
            partners[b],
        )
        for b in range(LEVELS)
    ]

    def ends(hh, s, p):
        below = at(hh, (z + NZ - s) % NZ, c)
        above = at(hh, (z + s) % NZ, c)
        return (below, above) if p % 2 == 0 else (above, below)

    def targets(p):
        return (up, down) if p % 2 == 0 else (down, up)

    def begin():
        for p in range(PASSES):
            long, short = targets(p)
            push(me, p, z_send.at[p], zsem(0, 1, p), long)
            push(me, p, z_send.at[p], zsem(1, 1, p), short)
        for p in range(PASSES):
            push(me, p, x_send.at[p], xsem(0, 0, p), across)
        for p in range(PASSES):
            to_sib(me, p)

    def ring(s):
        for p in range(PASSES):
            one, two = ends(h, s, p)
            long, short = targets(p)
            got(one, p, zsem(0, s, p))

            @pl.when(s < NZ // 2)
            def _(p=p, one=one, long=long):
                push(one, p, z_send.at[p], zsem(0, s + 1, p), long)

            push(one, p, x_send.at[p], xsem(0, s, p), across)
            to_sib(one, p)

            @pl.when(s < NZ // 2)
            def _(p=p, two=two, short=short):
                got(two, p, zsem(1, s, p))

                @pl.when(s < NZ // 2 - 1)
                def _():
                    push(two, p, z_send.at[p], zsem(1, s + 1, p), short)

                push(two, p, x_send.at[p], xsem(1, s, p), across)
                to_sib(two, p)

    def crossed(lo, hi):
        if lo == 0:
            for p in range(PASSES):
                got(across, p, xsem(0, 0, p))
                to_sib(across, p)

        def one(s, carry):
            for p in range(PASSES):
                first, second = ends(1 - h, s, p)
                got(first, p, xsem(0, s, p))
                to_sib(first, p)

                @pl.when(s < NZ // 2)
                def _(p=p, second=second):
                    got(second, p, xsem(1, s, p))
                    to_sib(second, p)

            return carry

        lax.fori_loop(max(lo, 1), hi, one, 0)

    begin()
    e1[0].start()
    load_gain.wait()
    normalise(x1, 0, RUN)

    def step(i, carry):
        ring(i)
        for b in range(1, LEVELS):

            @pl.when(i == EXCHANGE_AT[b - 1])
            def _(b=b):
                e1[b].start()

        return carry

    lax.fori_loop(1, NZ // 2 + 1, step, 0)
    crossed(0, 5)

    qrow = lax.broadcasted_iota(jnp.int32, (RUN, ROWS), 0)
    kcol = lax.broadcasted_iota(jnp.int32, (RUN, ROWS), 1)
    seen = (kcol >= RUN) | ((kcol >= BLOCK) == (qrow >= BLOCK))
    mask = jnp.where(seen, 1.0, 0.0).astype(jnp.float32)

    def unit(a):
        ms = jnp.mean(a * a, axis=-1, keepdims=True)
        return (a * lax.rsqrt(ms + EPS)).astype(jnp.bfloat16)

    scale = HEAD ** (-0.5)

    def lanes_of(p, i):
        return pl.ds(pl.multiple_of(p * PW + i * HEAD, HEAD), HEAD)

    def prepare(p, start, count, queries):
        base = pl.multiple_of(p * PCOLS, PCOLS)
        if queries:
            q = jnp.dot(
                nrm[pl.ds(0, RUN), :], wbuf[:, pl.ds(base, PW)], preferred_element_type=jnp.float32
            )
            for i in range(PW // HEAD):
                qn[:, lanes_of(p, i)] = unit(q[:, i * HEAD : (i + 1) * HEAD])
        part = nrm[pl.ds(start, count), :]
        k = jnp.dot(part, wbuf[:, pl.ds(base + PW, PW)], preferred_element_type=jnp.float32)
        v = jnp.dot(part, wbuf[:, pl.ds(base + 2 * PW, PW)], preferred_element_type=jnp.float32)
        for i in range(PW // HEAD):
            kn[pl.ds(start, count), lanes_of(p, i)] = unit(k[:, i * HEAD : (i + 1) * HEAD])
        vb[pl.ds(start, count), pl.ds(pl.multiple_of(p * PW, PW), PW)] = v.astype(jnp.bfloat16)

    def attend(p):
        for i in range(PW // HEAD):
            lanes = lanes_of(p, i)
            score = lax.dot_general(
                qn[:, lanes],
                kn[:, lanes],
                (((1,), (1,)), ((), ())),
                preferred_element_type=jnp.float32,
            )
            e = jnp.exp(score * scale) * mask
            weight = (e / jnp.sum(e, axis=-1, keepdims=True)).astype(jnp.bfloat16)
            att[:, lanes] = jnp.dot(
                weight, vb[:, lanes], preferred_element_type=jnp.float32
            ).astype(jnp.bfloat16)

    def project(xr, outv, part):
        def one(n, carry):
            lanes = pl.ds(pl.multiple_of(part * PART + n * PW, PW), PW)
            outv[:, lanes] = (
                xr[pl.ds(0, RUN), lanes].astype(jnp.float32)
                + jnp.dot(att[...], wo[:, lanes], preferred_element_type=jnp.float32)
            ).astype(jnp.bfloat16)
            return carry

        lax.fori_loop(0, PART // PW, one, 0)

    def tick_one(p):
        half = wbuf.at[pl.ds(0, 512), cols(p)]
        pltpu.make_async_copy(half, half, sib_recv.at[p]).wait()
        prepare(p, 0, ROWS, True)
        attend(p)

    for b in range(LEVELS):
        e1[b].wait_recv()
    normalise(x1, RUN, ROWS - RUN)
    crossed(5, NZ // 2 + 1)
    for p in range(PASSES):
        tick_one(p)
    load_wo.wait()
    load_arr.wait()
    o1 = out_ref.at[0, 0]
    relay, e2 = [], []
    for part in range(PARTS):
        lanes = pl.ds(part * PART, PART)
        sem = part * (LEVELS + 1)
        relay.append(
            exch(
                0,
                rbuf.at[:, lanes],
                x2.at[pl.ds(0, RUN), lanes],
                r_send.at[sem + LEVELS],
                r_recv.at[sem + LEVELS],
                nxt,
                me,
            )
        )
        e2.append(
            [
                exch(
                    b,
                    send2.at[b, :, lanes],
                    x2.at[pl.ds(RUN + b * BLOCK, BLOCK), lanes],
                    r_send.at[sem + b],
                    r_recv.at[sem + b],
                    sec if b < NEAR else nxt,
                    partners[b],
                )
                for b in range(LEVELS)
            ]
        )
    for part in range(PARTS):
        lanes = pl.ds(part * PART, PART)
        project(x1, o1, part)
        rbuf[:, lanes] = jnp.where(sec == sections - 1, arr[:, lanes], o1[:, lanes])
        for b in range(NEAR, LEVELS):
            send2[b, :, lanes] = choose(rbuf, partners[b], b, lanes)
        relay[part].start()
        for b in range(LEVELS - 1, NEAR - 1, -1):
            e2[part][b].start()
    for part in range(PARTS):
        lanes = pl.ds(part * PART, PART)
        relay[part].wait_recv()
        for b in range(NEAR - 1, -1, -1):
            send2[b, :, lanes] = choose(x2, partners[b], b, lanes)
            e2[part][b].start()
    EARLY = RUN + BLOCK
    for part in range(PARTS):
        e2[part][0].wait_recv()
    normalise(x2, 0, EARLY)

    def early(p, carry):
        prepare(p, 0, EARLY, True)
        return carry

    lax.fori_loop(0, PASSES, early, 0)
    for b in range(1, LEVELS):
        for part in range(PARTS):
            e2[part][b].wait_recv()
    normalise(x2, EARLY, ROWS - EARLY)

    def late(p, carry):
        prepare(p, EARLY, ROWS - EARLY, False)
        attend(p)
        return carry

    lax.fori_loop(0, PASSES, late, 0)
    for part in range(PARTS):
        project(x2, out_ref.at[1, 0], part)

    for p in range(PASSES):
        for n, sem in ((NZ - 1, z_send.at[p]), (NZ, x_send.at[p]), (2 * NZ, sib_send.at[p])):
            ref = wbuf.at[pl.ds(0, n * SHARD), cols(p)]
            pltpu.make_async_copy(ref, ref, sem).wait()
    for b in range(LEVELS):
        e1[b].wait_send()
        for part in range(PARTS):
            e2[part][b].wait_send()
    for part in range(PARTS):
        relay[part].wait_send()


def per_device(sections, x, arr, gain, w, wo, table):
    import functools

    anyspec = pl.BlockSpec(memory_space=pl.ANY)
    dma = pltpu.SemaphoreType.DMA
    bf = jnp.bfloat16
    return pl.pallas_call(
        functools.partial(kernel, sections),
        out_shape=jax.ShapeDtypeStruct((2, 1, RUN, D), bf),
        in_specs=[anyspec] * 6,
        out_specs=pl.BlockSpec(memory_space=pltpu.VMEM),
        scratch_shapes=[
            pltpu.VMEM((D, 3 * INNER), bf),
            pltpu.VMEM((INNER, D), bf),
            pltpu.VMEM((ROWS, D), bf),
            pltpu.VMEM((ROWS, D), bf),
            pltpu.VMEM((RUN, D), bf),
            pltpu.VMEM((ROWS, D), bf),
            pltpu.VMEM((RUN, INNER), bf),
            pltpu.VMEM((ROWS, INNER), bf),
            pltpu.VMEM((ROWS, INNER), bf),
            pltpu.VMEM((RUN, INNER), bf),
            pltpu.VMEM((1, D), jnp.float32),
            pltpu.VMEM(table.shape[::-1], jnp.int32),
            pltpu.VMEM((LEVELS, BLOCK, D), bf),
            pltpu.VMEM((LEVELS, BLOCK, D), bf),
            pltpu.VMEM((RUN, D), bf),
            dma((17,)),
            dma((2 * 9 * PASSES,)),
            dma((2 * 9 * PASSES,)),
            dma((PASSES,)),
            dma((PASSES,)),
            dma((PASSES,)),
            dma((PASSES,)),
            dma((LEVELS,)),
            dma((LEVELS,)),
            dma((PARTS * (LEVELS + 1),)),
            dma((PARTS * (LEVELS + 1),)),
        ],
        compiler_params=pltpu.CompilerParams(
            collective_id=0, has_side_effects=True, vmem_limit_bytes=24 * 1024 * 1024
        ),
    )(*[pltpu.with_memory_space_constraint(a, pltpu.HBM) for a in (x, arr, gain, w, wo, table.T)])


def solution(mesh):
    import functools

    placed = (
        P("section", "seq", None),
        P("seq", None),
        P("section", None),
        P("section", "seq", None),
        P("section", None, None),
        P(),
    )
    return jax.shard_map(
        functools.partial(per_device, mesh.shape["section"]),
        mesh=mesh,
        in_specs=placed,
        out_specs=P(None, "section", "seq", None),
        check_vma=False,
    )
```

```python
import jax
import jax.numpy as jnp
from jax import lax
from jax.experimental import pallas as pl
from jax.experimental.pallas import tpu as pltpu
from jax.sharding import PartitionSpec as P

HEADS = 8
HEAD = 128
BLOCK = 64
LEVELS = 4
NZ = 16
RUN = 128
D = 1024
INNER = 1024
SHARD = 16
PASSES = 4
PCOLS = 768
PW = 256
ROWS = RUN + LEVELS * BLOCK
EPS = 1e-06
NEAR = 2
PARTS = 2
PART = D // PARTS

EXCHANGE_AT = (5, 5, 5)


def flip(i, bit):
    step = 1 << bit
    return i + step * (1 - 2 * ((i // step) % 2))


def kernel(
    sections,
    x_hbm,
    arr_hbm,
    gain_hbm,
    w_hbm,
    wo_hbm,
    table_hbm,
    out_ref,
    wbuf,
    wo,
    x1,
    x2,
    arr,
    nrm,
    qn,
    kn,
    vb,
    att,
    gain_ref,
    table_ref,
    send1,
    send2,
    rbuf,
    load_sem,
    z_recv,
    x_recv,
    sib_recv,
    z_send,
    x_send,
    sib_send,
    e_send,
    e_recv,
    r_send,
    r_recv,
):
    sec = lax.axis_index("section")
    me = lax.axis_index("seq")
    h = me // (2 * NZ)
    z = (me // 2) % NZ
    c = me % 2
    nxt = (sec + 1) % sections
    prv = (sec + sections - 1) % sections

    def at(hh, zz, cc):
        return hh * (2 * NZ) + zz * 2 + cc

    up = at(h, (z + 1) % NZ, c)
    down = at(h, (z + NZ - 1) % NZ, c)
    sib = flip(me, 0)
    across = at(1 - h, z, c)
    partners = [flip(me, b) for b in range(LEVELS)]

    def dev(s, j):
        return {"section": s, "seq": j}

    barrier = pltpu.get_barrier_semaphore()
    talk = [(sec, up), (sec, down), (sec, sib), (sec, across)]
    talk += [(sec, partners[b]) for b in range(1, LEVELS)]
    talk += [(prv, me)] + [(prv, partners[b]) for b in range(NEAR, LEVELS)]
    for s, j in talk:
        pl.semaphore_signal(barrier, inc=1, device_id=dev(s, j))

    def choose(ref, reader, level, lanes):
        row = table_ref[pl.ds(level, 1), :].astype(jnp.float32)
        here = lax.broadcasted_iota(jnp.int32, row.shape, 1) == reader
        entry = jnp.sum(jnp.where(here, row, 0.0), axis=1, keepdims=True)
        lower = ref[pl.ds(0, BLOCK), lanes].astype(jnp.float32)
        upper = ref[pl.ds(BLOCK, BLOCK), lanes].astype(jnp.float32)
        second = jnp.broadcast_to(entry, lower.shape) > 0.5
        return jnp.where(second, upper, lower).astype(jnp.bfloat16)

    def rows(slot):
        return pl.ds(pl.multiple_of(slot * SHARD, SHARD), SHARD)

    loads = []
    for p in range(PASSES):
        for g in range(3):
            loads.append(
                pltpu.make_async_copy(
                    w_hbm.at[0, :, pl.ds(g * INNER + p * PW, PW)],
                    wbuf.at[rows(me), pl.ds(p * PCOLS + g * PW, PW)],
                    load_sem.at[p * 3 + g],
                )
            )
    load_x = pltpu.make_async_copy(x_hbm.at[0], x1.at[pl.ds(0, RUN)], load_sem.at[12])
    load_arr = pltpu.make_async_copy(arr_hbm, arr, load_sem.at[13])
    load_wo = pltpu.make_async_copy(wo_hbm.at[0], wo, load_sem.at[14])
    load_gain = pltpu.make_async_copy(gain_hbm, gain_ref, load_sem.at[15])
    load_table = pltpu.make_async_copy(table_hbm, table_ref, load_sem.at[16])
    load_table.start()
    load_x.start()
    load_gain.start()
    for cp in loads:
        cp.start()
    load_arr.start()
    load_wo.start()
    load_table.wait()
    load_x.wait()
    for b in range(LEVELS):
        send1[b] = choose(x1, partners[b], b, slice(None))
    for cp in loads:
        cp.wait()
    pl.semaphore_wait(barrier, len(talk))

    def normalise(xr, start, count):
        wide = xr[pl.ds(start, count), :].astype(jnp.float32)
        ms = jnp.mean(wide * wide, axis=-1, keepdims=True)
        nrm[pl.ds(start, count), :] = (wide * lax.rsqrt(ms + EPS) * gain_ref[...]).astype(
            jnp.bfloat16
        )

    def cols(p):
        return pl.ds(p * PCOLS, PCOLS)

    def piece(slot, p):
        return wbuf.at[rows(slot), cols(p)]

    def push(slot, p, send, recv, target):
        pltpu.make_async_remote_copy(
            src_ref=piece(slot, p),
            dst_ref=piece(slot, p),
            send_sem=send,
            recv_sem=recv,
            device_id=dev(sec, target),
        ).start()

    def got(slot, p, recv):
        pltpu.make_async_copy(piece(slot, p), piece(slot, p), recv).wait()

    def to_sib(slot, p):
        push(slot, p, sib_send.at[p], sib_recv.at[p], sib)

    def zsem(d, s, p):
        return z_recv.at[(d * 9 + s) * PASSES + p]

    def xsem(d, s, p):
        return x_recv.at[(d * 9 + s) * PASSES + p]

    def exch(b, src, dst, send, recv, s, j):
        return pltpu.make_async_remote_copy(
            src_ref=src, dst_ref=dst, send_sem=send, recv_sem=recv, device_id=dev(s, j)
        )

    e1 = [
        exch(
            b,
            send1.at[b],
            x1.at[pl.ds(RUN + b * BLOCK, BLOCK)],
            e_send.at[b],
            e_recv.at[b],
            sec,
            partners[b],
        )
        for b in range(LEVELS)
    ]

    def ends(hh, s, p):
        below = at(hh, (z + NZ - s) % NZ, c)
        above = at(hh, (z + s) % NZ, c)
        return (below, above) if p % 2 == 0 else (above, below)

    def targets(p):
        return (up, down) if p % 2 == 0 else (down, up)

    def begin():
        for p in range(PASSES):
            long, short = targets(p)
            push(me, p, z_send.at[p], zsem(0, 1, p), long)
            push(me, p, z_send.at[p], zsem(1, 1, p), short)
        for p in range(PASSES):
            push(me, p, x_send.at[p], xsem(0, 0, p), across)
        for p in range(PASSES):
            to_sib(me, p)

    def ring(s):
        for p in range(PASSES):
            one, two = ends(h, s, p)
            long, short = targets(p)
            got(one, p, zsem(0, s, p))

            @pl.when(s < NZ // 2)
            def _(p=p, one=one, long=long):
                push(one, p, z_send.at[p], zsem(0, s + 1, p), long)

            push(one, p, x_send.at[p], xsem(0, s, p), across)
            to_sib(one, p)

            @pl.when(s < NZ // 2)
            def _(p=p, two=two, short=short):
                got(two, p, zsem(1, s, p))

                @pl.when(s < NZ // 2 - 1)
                def _():
                    push(two, p, z_send.at[p], zsem(1, s + 1, p), short)

                push(two, p, x_send.at[p], xsem(1, s, p), across)
                to_sib(two, p)

    def crossed(lo, hi):
        if lo == 0:
            for p in range(PASSES):
                got(across, p, xsem(0, 0, p))
                to_sib(across, p)

        def one(s, carry):
            for p in range(PASSES):
                first, second = ends(1 - h, s, p)
                got(first, p, xsem(0, s, p))
                to_sib(first, p)

                @pl.when(s < NZ // 2)
                def _(p=p, second=second):
                    got(second, p, xsem(1, s, p))
                    to_sib(second, p)

            return carry

        lax.fori_loop(max(lo, 1), hi, one, 0)

    begin()
    e1[0].start()
    load_gain.wait()
    normalise(x1, 0, RUN)

    def step(i, carry):
        ring(i)
        for b in range(1, LEVELS):

            @pl.when(i == EXCHANGE_AT[b - 1])
            def _(b=b):
                e1[b].start()

        return carry

    lax.fori_loop(1, NZ // 2 + 1, step, 0)
    crossed(0, 5)

    qrow = lax.broadcasted_iota(jnp.int32, (RUN, RUN), 0)
    kcol = lax.broadcasted_iota(jnp.int32, (RUN, RUN), 1)
    mask = jnp.where((kcol >= BLOCK) == (qrow >= BLOCK), 1.0, 0.0).astype(jnp.float32)

    def unit(a):
        ms = jnp.mean(a * a, axis=-1, keepdims=True)
        return (a * lax.rsqrt(ms + EPS)).astype(jnp.bfloat16)

    scale = HEAD ** (-0.5)

    def lanes_of(p, i):
        return pl.ds(pl.multiple_of(p * PW + i * HEAD, HEAD), HEAD)

    def prepare(p, start, count, queries):
        base = pl.multiple_of(p * PCOLS, PCOLS)
        if queries:
            q = jnp.dot(
                nrm[pl.ds(0, RUN), :], wbuf[:, pl.ds(base, PW)], preferred_element_type=jnp.float32
            )
            for i in range(PW // HEAD):
                qn[:, lanes_of(p, i)] = unit(q[:, i * HEAD : (i + 1) * HEAD])
        part = nrm[pl.ds(start, count), :]
        k = jnp.dot(part, wbuf[:, pl.ds(base + PW, PW)], preferred_element_type=jnp.float32)
        v = jnp.dot(part, wbuf[:, pl.ds(base + 2 * PW, PW)], preferred_element_type=jnp.float32)
        for i in range(PW // HEAD):
            kn[pl.ds(start, count), lanes_of(p, i)] = unit(k[:, i * HEAD : (i + 1) * HEAD])
        vb[pl.ds(start, count), pl.ds(pl.multiple_of(p * PW, PW), PW)] = v.astype(jnp.bfloat16)

    def attend(p):
        for i in range(PW // HEAD):
            lanes = lanes_of(p, i)
            score = lax.dot_general(
                qn[:, lanes],
                kn[:, lanes],
                (((1,), (1,)), ((), ())),
                preferred_element_type=jnp.float32,
            )
            e = jnp.exp(score * scale)
            e = jnp.concatenate([e[:, :RUN] * mask, e[:, RUN:]], axis=1)
            share = 1.0 / jnp.sum(e, axis=-1, keepdims=True)
            weight = (e * share).astype(jnp.bfloat16)
            att[:, lanes] = jnp.dot(
                weight, vb[:, lanes], preferred_element_type=jnp.float32
            ).astype(jnp.bfloat16)

    def project(xr, outv, part):
        def one(n, carry):
            lanes = pl.ds(pl.multiple_of(part * PART + n * PW, PW), PW)
            outv[:, lanes] = (
                xr[pl.ds(0, RUN), lanes].astype(jnp.float32)
                + jnp.dot(att[...], wo[:, lanes], preferred_element_type=jnp.float32)
            ).astype(jnp.bfloat16)
            return carry

        lax.fori_loop(0, PART // PW, one, 0)

    def tick_one(p):
        half = wbuf.at[pl.ds(0, 512), cols(p)]
        pltpu.make_async_copy(half, half, sib_recv.at[p]).wait()
        prepare(p, 0, ROWS, True)
        attend(p)

    for b in range(LEVELS):
        e1[b].wait_recv()
    normalise(x1, RUN, ROWS - RUN)
    crossed(5, NZ // 2 + 1)
    for p in range(PASSES):
        tick_one(p)
    load_wo.wait()
    load_arr.wait()
    o1 = out_ref.at[0, 0]
    relay, e2 = [], []
    for part in range(PARTS):
        lanes = pl.ds(part * PART, PART)
        sem = part * (LEVELS + 1)
        relay.append(
            exch(
                0,
                rbuf.at[:, lanes],
                x2.at[pl.ds(0, RUN), lanes],
                r_send.at[sem + LEVELS],
                r_recv.at[sem + LEVELS],
                nxt,
                me,
            )
        )
        e2.append(
            [
                exch(
                    b,
                    send2.at[b, :, lanes],
                    x2.at[pl.ds(RUN + b * BLOCK, BLOCK), lanes],
                    r_send.at[sem + b],
                    r_recv.at[sem + b],
                    sec if b < NEAR else nxt,
                    partners[b],
                )
                for b in range(LEVELS)
            ]
        )
    for part in range(PARTS):
        lanes = pl.ds(part * PART, PART)
        project(x1, o1, part)
        rbuf[:, lanes] = jnp.where(sec == sections - 1, arr[:, lanes], o1[:, lanes])
        for b in range(NEAR, LEVELS):
            send2[b, :, lanes] = choose(rbuf, partners[b], b, lanes)
        relay[part].start()
        for b in range(LEVELS - 1, NEAR - 1, -1):
            e2[part][b].start()
    for part in range(PARTS):
        lanes = pl.ds(part * PART, PART)
        relay[part].wait_recv()
        for b in range(NEAR - 1, -1, -1):
            send2[b, :, lanes] = choose(x2, partners[b], b, lanes)
            e2[part][b].start()
    EARLY = RUN + BLOCK
    for part in range(PARTS):
        e2[part][0].wait_recv()
    normalise(x2, 0, EARLY)

    def early(p, carry):
        prepare(p, 0, EARLY, True)
        return carry

    lax.fori_loop(0, PASSES, early, 0)
    for b in range(1, LEVELS):
        for part in range(PARTS):
            e2[part][b].wait_recv()
        normalise(x2, RUN + b * BLOCK, BLOCK)

    def late(p, carry):
        prepare(p, EARLY, ROWS - EARLY, False)
        attend(p)
        return carry

    lax.fori_loop(0, PASSES, late, 0)
    for part in range(PARTS):
        project(x2, out_ref.at[1, 0], part)

    for p in range(PASSES):
        for n, sem in ((NZ - 1, z_send.at[p]), (NZ, x_send.at[p]), (2 * NZ, sib_send.at[p])):
            ref = wbuf.at[pl.ds(0, n * SHARD), cols(p)]
            pltpu.make_async_copy(ref, ref, sem).wait()
    for b in range(LEVELS):
        e1[b].wait_send()
        for part in range(PARTS):
            e2[part][b].wait_send()
    for part in range(PARTS):
        relay[part].wait_send()


def per_device(sections, x, arr, gain, w, wo, table):
    import functools

    anyspec = pl.BlockSpec(memory_space=pl.ANY)
    dma = pltpu.SemaphoreType.DMA
    bf = jnp.bfloat16
    return pl.pallas_call(
        functools.partial(kernel, sections),
        out_shape=jax.ShapeDtypeStruct((2, 1, RUN, D), bf),
        in_specs=[anyspec] * 6,
        out_specs=pl.BlockSpec(memory_space=pltpu.VMEM),
        scratch_shapes=[
            pltpu.VMEM((D, 3 * INNER), bf),
            pltpu.VMEM((INNER, D), bf),
            pltpu.VMEM((ROWS, D), bf),
            pltpu.VMEM((ROWS, D), bf),
            pltpu.VMEM((RUN, D), bf),
            pltpu.VMEM((ROWS, D), bf),
            pltpu.VMEM((RUN, INNER), bf),
            pltpu.VMEM((ROWS, INNER), bf),
            pltpu.VMEM((ROWS, INNER), bf),
            pltpu.VMEM((RUN, INNER), bf),
            pltpu.VMEM((1, D), jnp.float32),
            pltpu.VMEM(table.shape[::-1], jnp.int32),
            pltpu.VMEM((LEVELS, BLOCK, D), bf),
            pltpu.VMEM((LEVELS, BLOCK, D), bf),
            pltpu.VMEM((RUN, D), bf),
            dma((17,)),
            dma((2 * 9 * PASSES,)),
            dma((2 * 9 * PASSES,)),
            dma((PASSES,)),
            dma((PASSES,)),
            dma((PASSES,)),
            dma((PASSES,)),
            dma((LEVELS,)),
            dma((LEVELS,)),
            dma((PARTS * (LEVELS + 1),)),
            dma((PARTS * (LEVELS + 1),)),
        ],
        compiler_params=pltpu.CompilerParams(
            collective_id=0, has_side_effects=True, vmem_limit_bytes=24 * 1024 * 1024
        ),
    )(*[pltpu.with_memory_space_constraint(a, pltpu.HBM) for a in (x, arr, gain, w, wo, table.T)])


def solution(mesh):
    import functools

    placed = (
        P("section", "seq", None),
        P("seq", None),
        P("section", None),
        P("section", "seq", None),
        P("section", None, None),
        P(),
    )
    return jax.shard_map(
        functools.partial(per_device, mesh.shape["section"]),
        mesh=mesh,
        in_specs=placed,
        out_specs=P(None, "section", "seq", None),
        check_vma=False,
    )
```

```python
import jax
import jax.numpy as jnp
from jax import lax
from jax.experimental import pallas as pl
from jax.experimental.pallas import tpu as pltpu
from jax.sharding import PartitionSpec as P

HEADS = 8
HEAD = 128
BLOCK = 64
LEVELS = 4
NZ = 16
RUN = 128
D = 1024
INNER = 1024
SHARD = 16
PASSES = 4
PCOLS = 768
PW = 256
ROWS = RUN + LEVELS * BLOCK
EPS = 1e-06
NEAR = 2
PARTS = 2
PART = D // PARTS

EXCHANGE_AT = (6, 6, 6)


def flip(i, bit):
    step = 1 << bit
    return i + step * (1 - 2 * ((i // step) % 2))


def kernel(
    sections,
    x_hbm,
    arr_hbm,
    gain_hbm,
    w_hbm,
    wo_hbm,
    table_hbm,
    out_ref,
    wbuf,
    wo,
    x1,
    x2,
    arr,
    nrm,
    qn,
    kn,
    vb,
    att,
    gain_ref,
    table_ref,
    send1,
    send2,
    rbuf,
    load_sem,
    z_recv,
    x_recv,
    sib_recv,
    z_send,
    x_send,
    sib_send,
    e_send,
    e_recv,
    r_send,
    r_recv,
):
    sec = lax.axis_index("section")
    me = lax.axis_index("seq")
    h = me // (2 * NZ)
    z = (me // 2) % NZ
    c = me % 2
    nxt = (sec + 1) % sections
    prv = (sec + sections - 1) % sections

    def at(hh, zz, cc):
        return hh * (2 * NZ) + zz * 2 + cc

    up = at(h, (z + 1) % NZ, c)
    down = at(h, (z + NZ - 1) % NZ, c)
    sib = flip(me, 0)
    across = at(1 - h, z, c)
    partners = [flip(me, b) for b in range(LEVELS)]

    def dev(s, j):
        return {"section": s, "seq": j}

    barrier = pltpu.get_barrier_semaphore()
    talk = [(sec, up), (sec, down), (sec, sib), (sec, across)]
    talk += [(sec, partners[b]) for b in range(1, LEVELS)]
    talk += [(prv, me)] + [(prv, partners[b]) for b in range(NEAR, LEVELS)]
    for s, j in talk:
        pl.semaphore_signal(barrier, inc=1, device_id=dev(s, j))

    def choose(ref, reader, level, lanes):
        row = table_ref[pl.ds(level, 1), :].astype(jnp.float32)
        here = lax.broadcasted_iota(jnp.int32, row.shape, 1) == reader
        entry = jnp.sum(jnp.where(here, row, 0.0), axis=1, keepdims=True)
        lower = ref[pl.ds(0, BLOCK), lanes].astype(jnp.float32)
        upper = ref[pl.ds(BLOCK, BLOCK), lanes].astype(jnp.float32)
        second = jnp.broadcast_to(entry, lower.shape) > 0.5
        return jnp.where(second, upper, lower).astype(jnp.bfloat16)

    def rows(slot):
        return pl.ds(pl.multiple_of(slot * SHARD, SHARD), SHARD)

    loads = []
    for p in range(PASSES):
        for g in range(3):
            loads.append(
                pltpu.make_async_copy(
                    w_hbm.at[0, :, pl.ds(g * INNER + p * PW, PW)],
                    wbuf.at[rows(me), pl.ds(p * PCOLS + g * PW, PW)],
                    load_sem.at[p * 3 + g],
                )
            )
    load_x = pltpu.make_async_copy(x_hbm.at[0], x1.at[pl.ds(0, RUN)], load_sem.at[12])
    load_arr = pltpu.make_async_copy(arr_hbm, arr, load_sem.at[13])
    load_wo = pltpu.make_async_copy(wo_hbm.at[0], wo, load_sem.at[14])
    load_gain = pltpu.make_async_copy(gain_hbm, gain_ref, load_sem.at[15])
    load_table = pltpu.make_async_copy(table_hbm, table_ref, load_sem.at[16])
    load_table.start()
    load_x.start()
    load_gain.start()
    for cp in loads:
        cp.start()
    load_arr.start()
    load_wo.start()
    load_table.wait()
    load_x.wait()
    for b in range(LEVELS):
        send1[b] = choose(x1, partners[b], b, slice(None))
    for cp in loads:
        cp.wait()
    pl.semaphore_wait(barrier, len(talk))

    def normalise(xr, start, count):
        wide = xr[pl.ds(start, count), :].astype(jnp.float32)
        ms = jnp.mean(wide * wide, axis=-1, keepdims=True)
        nrm[pl.ds(start, count), :] = (wide * lax.rsqrt(ms + EPS) * gain_ref[...]).astype(
            jnp.bfloat16
        )

    def cols(p):
        return pl.ds(p * PCOLS, PCOLS)

    def piece(slot, p):
        return wbuf.at[rows(slot), cols(p)]

    def push(slot, p, send, recv, target):
        pltpu.make_async_remote_copy(
            src_ref=piece(slot, p),
            dst_ref=piece(slot, p),
            send_sem=send,
            recv_sem=recv,
            device_id=dev(sec, target),
        ).start()

    def got(slot, p, recv):
        pltpu.make_async_copy(piece(slot, p), piece(slot, p), recv).wait()

    def to_sib(slot, p):
        push(slot, p, sib_send.at[p], sib_recv.at[p], sib)

    def zsem(d, s, p):
        return z_recv.at[(d * 9 + s) * PASSES + p]

    def xsem(d, s, p):
        return x_recv.at[(d * 9 + s) * PASSES + p]

    def exch(b, src, dst, send, recv, s, j):
        return pltpu.make_async_remote_copy(
            src_ref=src, dst_ref=dst, send_sem=send, recv_sem=recv, device_id=dev(s, j)
        )

    e1 = [
        exch(
            b,
            send1.at[b],
            x1.at[pl.ds(RUN + b * BLOCK, BLOCK)],
            e_send.at[b],
            e_recv.at[b],
            sec,
            partners[b],
        )
        for b in range(LEVELS)
    ]

    def ends(hh, s, p):
        below = at(hh, (z + NZ - s) % NZ, c)
        above = at(hh, (z + s) % NZ, c)
        return (below, above) if p % 2 == 0 else (above, below)

    def targets(p):
        return (up, down) if p % 2 == 0 else (down, up)

    def begin():
        for p in range(PASSES):
            long, short = targets(p)
            push(me, p, z_send.at[p], zsem(0, 1, p), long)
            push(me, p, z_send.at[p], zsem(1, 1, p), short)
        for p in range(PASSES):
            push(me, p, x_send.at[p], xsem(0, 0, p), across)
        for p in range(PASSES):
            to_sib(me, p)

    def ring(s):
        for p in range(PASSES):
            one, two = ends(h, s, p)
            long, short = targets(p)
            got(one, p, zsem(0, s, p))

            @pl.when(s < NZ // 2)
            def _(p=p, one=one, long=long):
                push(one, p, z_send.at[p], zsem(0, s + 1, p), long)

            push(one, p, x_send.at[p], xsem(0, s, p), across)
            to_sib(one, p)

            @pl.when(s < NZ // 2)
            def _(p=p, two=two, short=short):
                got(two, p, zsem(1, s, p))

                @pl.when(s < NZ // 2 - 1)
                def _():
                    push(two, p, z_send.at[p], zsem(1, s + 1, p), short)

                push(two, p, x_send.at[p], xsem(1, s, p), across)
                to_sib(two, p)

    def crossed(lo, hi):
        if lo == 0:
            for p in range(PASSES):
                got(across, p, xsem(0, 0, p))
                to_sib(across, p)

        def one(s, carry):
            for p in range(PASSES):
                first, second = ends(1 - h, s, p)
                got(first, p, xsem(0, s, p))
                to_sib(first, p)

                @pl.when(s < NZ // 2)
                def _(p=p, second=second):
                    got(second, p, xsem(1, s, p))
                    to_sib(second, p)

            return carry

        lax.fori_loop(max(lo, 1), hi, one, 0)

    begin()
    e1[0].start()
    load_gain.wait()
    normalise(x1, 0, RUN)

    def step(i, carry):
        ring(i)
        for b in range(1, LEVELS):

            @pl.when(i == EXCHANGE_AT[b - 1])
            def _(b=b):
                e1[b].start()

        return carry

    lax.fori_loop(1, NZ // 2 + 1, step, 0)
    crossed(0, 5)

    qrow = lax.broadcasted_iota(jnp.int32, (RUN, ROWS), 0)
    kcol = lax.broadcasted_iota(jnp.int32, (RUN, ROWS), 1)
    seen = (kcol >= RUN) | ((kcol >= BLOCK) == (qrow >= BLOCK))
    mask = jnp.where(seen, 1.0, 0.0).astype(jnp.float32)

    def unit(a):
        ms = jnp.mean(a * a, axis=-1, keepdims=True)
        return (a * lax.rsqrt(ms + EPS)).astype(jnp.bfloat16)

    scale = HEAD ** (-0.5)

    def lanes_of(p, i):
        return pl.ds(pl.multiple_of(p * PW + i * HEAD, HEAD), HEAD)

    def prepare(p, start, count, queries):
        base = pl.multiple_of(p * PCOLS, PCOLS)
        if queries:
            q = jnp.dot(
                nrm[pl.ds(0, RUN), :], wbuf[:, pl.ds(base, PW)], preferred_element_type=jnp.float32
            )
            for i in range(PW // HEAD):
                qn[:, lanes_of(p, i)] = unit(q[:, i * HEAD : (i + 1) * HEAD])
        part = nrm[pl.ds(start, count), :]
        k = jnp.dot(part, wbuf[:, pl.ds(base + PW, PW)], preferred_element_type=jnp.float32)
        v = jnp.dot(part, wbuf[:, pl.ds(base + 2 * PW, PW)], preferred_element_type=jnp.float32)
        for i in range(PW // HEAD):
            kn[pl.ds(start, count), lanes_of(p, i)] = unit(k[:, i * HEAD : (i + 1) * HEAD])
        vb[pl.ds(start, count), pl.ds(pl.multiple_of(p * PW, PW), PW)] = v.astype(jnp.bfloat16)

    def attend(p):
        for i in range(PW // HEAD):
            lanes = lanes_of(p, i)
            score = lax.dot_general(
                qn[:, lanes],
                kn[:, lanes],
                (((1,), (1,)), ((), ())),
                preferred_element_type=jnp.float32,
            )
            e = jnp.exp(score * scale) * mask
            weight = (e / jnp.sum(e, axis=-1, keepdims=True)).astype(jnp.bfloat16)
            att[:, lanes] = jnp.dot(
                weight, vb[:, lanes], preferred_element_type=jnp.float32
            ).astype(jnp.bfloat16)

    def project(xr, outv, part):
        def one(n, carry):
            lanes = pl.ds(pl.multiple_of(part * PART + n * PW, PW), PW)
            outv[:, lanes] = (
                xr[pl.ds(0, RUN), lanes].astype(jnp.float32)
                + jnp.dot(att[...], wo[:, lanes], preferred_element_type=jnp.float32)
            ).astype(jnp.bfloat16)
            return carry

        lax.fori_loop(0, PART // PW, one, 0)

    def tick_one(p):
        half = wbuf.at[pl.ds(0, 512), cols(p)]
        pltpu.make_async_copy(half, half, sib_recv.at[p]).wait()
        prepare(p, 0, ROWS, True)
        attend(p)

    for b in range(LEVELS):
        e1[b].wait_recv()
    normalise(x1, RUN, ROWS - RUN)
    crossed(5, NZ // 2 + 1)
    for p in range(PASSES):
        tick_one(p)
    load_wo.wait()
    load_arr.wait()
    o1 = out_ref.at[0, 0]
    relay, e2 = [], []
    for part in range(PARTS):
        lanes = pl.ds(part * PART, PART)
        sem = part * (LEVELS + 1)
        relay.append(
            exch(
                0,
                rbuf.at[:, lanes],
                x2.at[pl.ds(0, RUN), lanes],
                r_send.at[sem + LEVELS],
                r_recv.at[sem + LEVELS],
                nxt,
                me,
            )
        )
        e2.append(
            [
                exch(
                    b,
                    send2.at[b, :, lanes],
                    x2.at[pl.ds(RUN + b * BLOCK, BLOCK), lanes],
                    r_send.at[sem + b],
                    r_recv.at[sem + b],
                    sec if b < NEAR else nxt,
                    partners[b],
                )
                for b in range(LEVELS)
            ]
        )
    for part in range(PARTS):
        lanes = pl.ds(part * PART, PART)
        project(x1, o1, part)
        rbuf[:, lanes] = jnp.where(sec == sections - 1, arr[:, lanes], o1[:, lanes])
        for b in range(NEAR, LEVELS):
            send2[b, :, lanes] = choose(rbuf, partners[b], b, lanes)
        relay[part].start()
        for b in range(LEVELS - 1, NEAR - 1, -1):
            e2[part][b].start()
    for part in range(PARTS):
        lanes = pl.ds(part * PART, PART)
        relay[part].wait_recv()
        for b in range(NEAR - 1, -1, -1):
            send2[b, :, lanes] = choose(x2, partners[b], b, lanes)
            e2[part][b].start()
    EARLY = RUN + BLOCK
    for part in range(PARTS):
        e2[part][0].wait_recv()
    normalise(x2, 0, EARLY)

    def early(p, carry):
        prepare(p, 0, EARLY, True)
        return carry

    lax.fori_loop(0, PASSES, early, 0)
    for b in range(1, LEVELS):
        for part in range(PARTS):
            e2[part][b].wait_recv()
    normalise(x2, EARLY, ROWS - EARLY)

    def late(p, carry):
        prepare(p, EARLY, ROWS - EARLY, False)
        attend(p)
        return carry

    lax.fori_loop(0, PASSES, late, 0)
    for part in range(PARTS):
        project(x2, out_ref.at[1, 0], part)

    for p in range(PASSES):
        for n, sem in ((NZ - 1, z_send.at[p]), (NZ, x_send.at[p]), (2 * NZ, sib_send.at[p])):
            ref = wbuf.at[pl.ds(0, n * SHARD), cols(p)]
            pltpu.make_async_copy(ref, ref, sem).wait()
    for b in range(LEVELS):
        e1[b].wait_send()
        for part in range(PARTS):
            e2[part][b].wait_send()
    for part in range(PARTS):
        relay[part].wait_send()


def per_device(sections, x, arr, gain, w, wo, table):
    import functools

    anyspec = pl.BlockSpec(memory_space=pl.ANY)
    dma = pltpu.SemaphoreType.DMA
    bf = jnp.bfloat16
    return pl.pallas_call(
        functools.partial(kernel, sections),
        out_shape=jax.ShapeDtypeStruct((2, 1, RUN, D), bf),
        in_specs=[anyspec] * 6,
        out_specs=pl.BlockSpec(memory_space=pltpu.VMEM),
        scratch_shapes=[
            pltpu.VMEM((D, 3 * INNER), bf),
            pltpu.VMEM((INNER, D), bf),
            pltpu.VMEM((ROWS, D), bf),
            pltpu.VMEM((ROWS, D), bf),
            pltpu.VMEM((RUN, D), bf),
            pltpu.VMEM((ROWS, D), bf),
            pltpu.VMEM((RUN, INNER), bf),
            pltpu.VMEM((ROWS, INNER), bf),
            pltpu.VMEM((ROWS, INNER), bf),
            pltpu.VMEM((RUN, INNER), bf),
            pltpu.VMEM((1, D), jnp.float32),
            pltpu.VMEM(table.shape[::-1], jnp.int32),
            pltpu.VMEM((LEVELS, BLOCK, D), bf),
            pltpu.VMEM((LEVELS, BLOCK, D), bf),
            pltpu.VMEM((RUN, D), bf),
            dma((17,)),
            dma((2 * 9 * PASSES,)),
            dma((2 * 9 * PASSES,)),
            dma((PASSES,)),
            dma((PASSES,)),
            dma((PASSES,)),
            dma((PASSES,)),
            dma((LEVELS,)),
            dma((LEVELS,)),
            dma((PARTS * (LEVELS + 1),)),
            dma((PARTS * (LEVELS + 1),)),
        ],
        compiler_params=pltpu.CompilerParams(
            collective_id=0, has_side_effects=True, vmem_limit_bytes=24 * 1024 * 1024
        ),
    )(*[pltpu.with_memory_space_constraint(a, pltpu.HBM) for a in (x, arr, gain, w, wo, table.T)])


def solution(mesh):
    import functools

    placed = (
        P("section", "seq", None),
        P("seq", None),
        P("section", None),
        P("section", "seq", None),
        P("section", None, None),
        P(),
    )
    return jax.shard_map(
        functools.partial(per_device, mesh.shape["section"]),
        mesh=mesh,
        in_specs=placed,
        out_specs=P(None, "section", "seq", None),
        check_vma=False,
    )
```
